512 devices in a mesh: narrow: 16 (over z), wide: 32 (over y, x, core).
Axes of the slice: x: 4, y: 4, z: 16, core: 2. Of those that a mesh axis runs over, the one named last changes fastest.
Arguments:
- sources: float32 [16, 64, 128, 256], P(None, 'wide', 'narrow')
- well_columns: int32 [16], replicated, may hold values from 0 to 8191
- column_active: int32 [64, 128], P('wide', 'narrow'), may hold values 0 or 1
- perm_root: float32 [64, 128, 256], P('wide', 'narrow'), may hold values from 0.5 to 2
- storage_term: float32 [64, 128, 256], P('wide', 'narrow'), may hold values from 0.2 to 2
- inverse_blocks: bfloat16 [64, 128, 2, 128, 128], P('wide', 'narrow')
Outputs:
- solution: float32 [16, 64, 128, 256], P(None, 'wide', 'narrow')
- residual: float32 [16, 64, 128, 256], P(None, 'wide', 'narrow')
The draws below stay inside these ranges and needn't reach their ends.
All inputs are finite; a program needn't handle non-finite values. No bound on the sum of `column_active` on one device may be relied on, other than what follows from the above.
Results may differ from the reference program's by a relative error of at most 0.0085.
Values sent between devices are 32-bit elements; how exact they have to be, the bound alone decides.
A program may use at most 64 MiB of HBM per device.

```python
import math
import jax
import jax.numpy as jnp
from jax import lax

K = 16
NZ = 256
BLK = 128
ITERS = 3
NX = 64
NY = 128
NB = 2


def draw_sources(key, part):
    first, second = jax.random.split(key, 2)
    shape = (K, NX, NY, NZ)
    positions = jnp.arange(NX, dtype=jnp.float32)
    rising = 1.0 + 2.0 * positions / max(NX - 1, 1)
    rough = jnp.exp(jax.random.uniform(second, shape, jnp.float32, -0.7, 0.7))
    core = jnp.clip(jax.random.normal(first, shape, jnp.float32), -6.0, 6.0)
    return 3.0 * core * rough * rising[None, :, None, None]


def draw_inverse_blocks(key, part):
    first, second = jax.random.split(key, 2)
    shape = (NX, NY, NZ // BLK, BLK, BLK)
    noise = jax.random.uniform(first, shape, jnp.float32, -1.0, 1.0)
    sym = 0.5 * (noise + jnp.swapaxes(noise, -1, -2))
    rows = jnp.arange(BLK, dtype=jnp.int32)
    ident = (rows[:, None] == rows[None, :]).astype(jnp.float32)
    diag_vals = 1.0 + 0.5 * jax.random.uniform(second, shape[:-1], jnp.float32)
    matrix = sym * (1.0 / BLK) * (1.0 - ident) + ident * diag_vals[..., None]
    return matrix.astype(jnp.bfloat16)


def with_ends(values, stream_key, smallest, largest):
    longest = values.shape.index(max(values.shape))
    spots = []
    for shift in (0, 1):
        where = [jax.random.randint(jax.random.fold_in(stream_key, axis), (), 0, length) for axis, length in enumerate(values.shape)]
        where[longest] = (where[longest] + shift) % values.shape[longest]
        spots.append(tuple(where))
    return values.at[spots[0]].set(smallest).at[spots[1]].set(largest)


def block_scale(own_key, shape, shards, least, high):
    def one(position, parts):
        steps = jax.random.uniform(jax.random.fold_in(jax.random.fold_in(own_key, 6), position), (parts,), jnp.float32, least / len(shards), high / len(shards))
        return jnp.repeat(jnp.exp(steps), shape[position] // parts).reshape((-1,) + (1,) * (len(shape) - position - 1))

    loudness = one(*shards[0])
    for cut in shards[1:]:
        loudness = loudness * one(*cut)
    return loudness


def setup_inputs(seed: int = 0) -> dict:
    splits = jax.random.split(jax.random.key(seed), 7)
    return {
        "sources": draw_sources(jax.random.fold_in(splits[6], 71), 0),
        "well_columns": with_ends(jax.random.randint(splits[1], (K,), 0, NX * NY), jax.random.fold_in(splits[1], 1), 0, (NX * NY) - 1).astype(jnp.int32),
        "column_active": with_ends((jax.random.randint(splits[2], (NX, NY), 0, 10) < 9).astype(jnp.int32), jax.random.fold_in(splits[2], 1), 0, 1),
        "perm_root": jnp.clip(jnp.exp(math.log(2.0) - 1.3862944 * jax.random.uniform(splits[3], (NX, NY, NZ), jnp.float32) ** block_scale(splits[3], (NX, NY, NZ), ((0, 32), (1, 16)), -0.2, 0.2)), 0.5, 2.0),
        "storage_term": jnp.clip(jnp.exp(math.log(2.0) - 2.3025851 * jax.random.uniform(splits[4], (NX, NY, NZ), jnp.float32) ** block_scale(splits[4], (NX, NY, NZ), ((0, 32), (1, 16)), -0.2, 0.2)), 0.2, 2.0),
        "inverse_blocks": draw_inverse_blocks(jax.random.fold_in(splits[6], 71), 0),
    }


WELL_RATE = 4.0

def coupling(padded, coef_pad):
    center = padded[:, 1:-1, 1:-1]
    coef = coef_pad[1:-1, 1:-1]
    total = coef_pad[2:, 1:-1] * (center - padded[:, 2:, 1:-1]) + coef_pad[:-2, 1:-1] * (center - padded[:, :-2, 1:-1])
    total = total + coef_pad[1:-1, 2:] * (center - padded[:, 1:-1, 2:]) + coef_pad[1:-1, :-2] * (center - padded[:, 1:-1, :-2])
    zero_layer = jnp.zeros_like(center[..., :1])
    zero_coef = jnp.zeros_like(coef[..., :1])
    upper = jnp.concatenate([center[..., 1:], zero_layer], -1)
    upper_coef = jnp.concatenate([coef[..., 1:], zero_coef], -1)
    lower = jnp.concatenate([zero_layer, center[..., :-1]], -1)
    lower_coef = jnp.concatenate([zero_coef, coef[..., :-1]], -1)
    total = total + upper_coef * (center - upper) + lower_coef * (center - lower)
    return coef * total

def operate(values, diag_term, coef_pad):
    padded = jnp.pad(values, ((0, 0), (1, 1), (1, 1), (0, 0)))
    return diag_term * values + coupling(padded, coef_pad)

def precondition(values, inverse_blocks):
    rounded = values.astype(jnp.bfloat16)
    rounded = lax.optimization_barrier(rounded).astype(jnp.float32)
    shaped = rounded.reshape(K, NX, NY, NB, BLK)
    moved = jnp.moveaxis(shaped, 1, 0)

    def one_row(pieces):
        return jnp.einsum('ybij,kybj->kybi', pieces[0].astype(jnp.float32), pieces[1], precision=lax.Precision.HIGHEST)
    output = lax.map(one_row, (inverse_blocks, moved))
    return jnp.moveaxis(output, 0, 1).reshape(K, NX, NY, NZ)

def gram_of(left, right):
    return jnp.einsum('kxyz,lxyz->kl', left, right, precision=lax.Precision.HIGHEST)

def combine(values, coefs):
    return jnp.einsum('kxyz,kl->lxyz', values, coefs, precision=lax.Precision.HIGHEST)

def solve_gram(matrix, target):
    sym = 0.5 * (matrix + matrix.T)
    factor = jnp.linalg.cholesky(sym)
    inner = lax.linalg.triangular_solve(factor, target, left_side=True, lower=True)
    return lax.linalg.triangular_solve(factor, inner, left_side=True, lower=True, transpose_a=True)

def reference(sources, well_columns, column_active, perm_root, storage_term, inverse_blocks):
    active = column_active.astype(jnp.float32)[..., None]
    coef = perm_root * active
    coef_pad = jnp.pad(coef, ((1, 1), (1, 1), (0, 0)))
    diag_term = active * storage_term + (1.0 - active)
    column_ids = jnp.arange(NX * NY, dtype=jnp.int32).reshape(NX, NY)
    wells = (column_ids[None] == well_columns[:, None, None]).astype(jnp.float32)
    residual = sources + WELL_RATE * wells[..., None]
    solution = jnp.zeros_like(residual)
    zset = precondition(residual, inverse_blocks)
    res_gram = gram_of(zset, residual)
    direction = zset
    for iteration in range(ITERS):
        image = operate(direction, diag_term, coef_pad)
        curv_gram = gram_of(direction, image)
        step_size = solve_gram(curv_gram, res_gram)
        solution = solution + combine(direction, step_size)
        residual = residual - combine(image, step_size)
        if iteration + 1 < ITERS:
            zset = precondition(residual, inverse_blocks)
            new_gram = gram_of(zset, residual)
            conj_coef = solve_gram(res_gram, new_gram)
            direction = zset + combine(direction, conj_coef)
            res_gram = new_gram
    return (solution, residual)
```

```python
import functools

import jax
import jax.numpy as jnp
from jax import lax
from jax.experimental import pallas as pl
from jax.experimental.pallas import tpu as pltpu
from jax.sharding import PartitionSpec as P

BASIS = 3
WELL_RATE = 4.0
BASIS_SCALE = 1.0 / 16.0
MESH = pl.DeviceIdType.MESH
EXACT = lax.Precision.HIGHEST
F32 = jnp.float32


def dot_nt(left, right):
    return lax.dot_general(left, right, (((1,), (1,)), ((), ())), precision=EXACT, preferred_element_type=F32)


def dot_nn(left, right):
    return lax.dot_general(left, right, (((1,), (0,)), ((), ())), precision=EXACT, preferred_element_type=F32)


def kernel(
    n_wide,
    n_narrow,
    src_hbm,
    wells_hbm,
    active_hbm,
    perm_hbm,
    storage_hbm,
    inv_hbm,
    sol_ref,
    res_ref,
    rhs,
    wells,
    active,
    perm,
    storage,
    inv,
    coef,
    coef_y,
    coef_x,
    coef_pad,
    diag,
    zs,
    ws,
    halo_x,
    halo_y,
    part,
    rows_in,
    plane_in,
    plane,
    all_rows,
    total,
    load_sem,
    coef_send,
    coef_recv,
    halo_send,
    halo_recv,
    sum_send,
    sum_recv,
):
    kk, cx, cy, nz = src_hbm.shape
    blk = inv_hbm.shape[-1]
    nb = inv_hbm.shape[2]
    me_w, me_n = lax.axis_index("wide"), lax.axis_index("narrow")
    right, left = lax.rem(me_w + 1, n_wide), lax.rem(me_w + n_wide - 1, n_wide)
    above, below = lax.rem(me_n + 1, n_narrow), lax.rem(me_n + n_narrow - 1, n_narrow)

    barrier = pltpu.get_barrier_semaphore()

    @pl.loop(1, n_narrow)
    def _(d):
        peer = lax.rem(me_n + d, n_narrow)
        pl.semaphore_signal(barrier, inc=1, device_id={"narrow": peer}, device_id_type=MESH)

    @pl.loop(1, n_wide)
    def _(d):
        peer = lax.rem(me_w + d, n_wide)
        pl.semaphore_signal(barrier, inc=1, device_id={"wide": peer}, device_id_type=MESH)

    loads = [
        pltpu.make_async_copy(wells_hbm, wells, load_sem.at[0]),
        pltpu.make_async_copy(active_hbm, active, load_sem.at[1]),
        pltpu.make_async_copy(perm_hbm, perm, load_sem.at[2]),
        pltpu.make_async_copy(storage_hbm, storage, load_sem.at[3]),
        pltpu.make_async_copy(inv_hbm, inv, load_sem.at[4]),
    ]
    columns = [(x, y) for x in range(cx) for y in range(cy)]
    for at, (x, y) in enumerate(columns):
        loads.append(pltpu.make_async_copy(src_hbm.at[:, x, y, :], rhs.at[x, y], load_sem.at[5 + at]))
    for load in loads:
        load.start()
    for load in loads[:4]:
        load.wait()

    row = lax.broadcasted_iota(jnp.int32, (cy, nz), 0)
    for x in range(cx):
        on = jnp.zeros((cy, nz), F32)
        for y in range(cy):
            on = jnp.where(row == y, active[x, y].astype(F32), on)
        coef[x] = perm[x] * on
        diag[x] = on * storage[x] + (1.0 - on)

    ids = lax.broadcasted_iota(jnp.int32, (kk, nz), 0)
    well_of = jnp.zeros((kk, nz), jnp.int32)
    for k in range(kk):
        well_of = jnp.where(ids == k, wells[k], well_of)
    for load in loads[4:]:
        load.wait()

    def precondition(get, put):
        for x, y in columns:
            value = get(x, y)
            high = value.astype(jnp.bfloat16)
            low = (value - high.astype(F32)).astype(jnp.bfloat16)
            both = jnp.concatenate([high, low], axis=0)
            for b in range(nb):
                out = lax.dot_general(
                    both[:, b * blk : (b + 1) * blk],
                    inv[x, y, b],
                    (((1,), (0,)), ((), ())),
                    preferred_element_type=F32,
                )
                put(x, y, b, out[:kk] + out[kk:])

    first_x, first_y = me_w * cx, me_n * cy
    for x, y in columns:
        here = (first_x + x) * (n_narrow * cy) + first_y + y
        rhs[x, y] = rhs[x, y] + jnp.where(well_of == here, WELL_RATE, 0.0)

    def store_z(i, scale):
        def put(x, y, b, value):
            zs[i, x, y, :, b * blk : (b + 1) * blk] = value * scale if scale != 1.0 else value

        return put

    precondition(lambda x, y: rhs[x, y], store_z(0, 1.0))

    pl.semaphore_wait(barrier, n_narrow + n_wide - 2)

    def remote(source, target, send, recv, device):
        return pltpu.make_async_remote_copy(
            src_ref=source, dst_ref=target, send_sem=send, recv_sem=recv, device_id=device, device_id_type=MESH
        )

    def send_halo(i):
        copies = [
            remote(zs.at[i, cx - 1], halo_x.at[i, 0], halo_send.at[i, 0], halo_recv.at[i, 0], {"wide": right}),
            remote(zs.at[i, 0], halo_x.at[i, 1], halo_send.at[i, 1], halo_recv.at[i, 1], {"wide": left}),
            remote(zs.at[i, :, cy - 1], halo_y.at[i, 0], halo_send.at[i, 2], halo_recv.at[i, 2], {"narrow": above}),
            remote(zs.at[i, :, 0], halo_y.at[i, 1], halo_send.at[i, 3], halo_recv.at[i, 3], {"narrow": below}),
        ]
        for copy in copies:
            copy.start()
        return copies

    coef_copies = [
        remote(coef.at[cx - 1], coef_x.at[0], coef_send.at[0], coef_recv.at[0], {"wide": right}),
        remote(coef.at[0], coef_x.at[1], coef_send.at[1], coef_recv.at[1], {"wide": left}),
        remote(coef, coef_y.at[0], coef_send.at[2], coef_recv.at[2], {"narrow": above}),
        remote(coef, coef_y.at[1], coef_send.at[3], coef_recv.at[3], {"narrow": below}),
    ]
    for copy in coef_copies:
        copy.start()
    flying = send_halo(0)

    has_left = jnp.where(me_w == 0, 0.0, 1.0)
    has_right = jnp.where(me_w == n_wide - 1, 0.0, 1.0)
    has_below = jnp.where(me_n == 0, 0.0, 1.0)
    has_above = jnp.where(me_n == n_narrow - 1, 0.0, 1.0)

    def spread(line):
        return jnp.broadcast_to(line, (8, nz))

    for x, y in columns:
        coef_pad[x + 1, y + 1] = spread(coef[x, y : y + 1])
    for copy in coef_copies:
        copy.wait()
    for y in range(cy):
        coef_pad[0, y + 1] = spread(coef_x[0, y : y + 1] * has_left)
        coef_pad[cx + 1, y + 1] = spread(coef_x[1, y : y + 1] * has_right)
    for x in range(cx):
        coef_pad[x + 1, 0] = spread(coef_y[0, x, cy - 1 : cy] * has_below)
        coef_pad[x + 1, cy + 1] = spread(coef_y[1, x, 0:1] * has_above)

    lane8 = lax.broadcasted_iota(jnp.int32, (8, nz), 1)

    def next_layer(value):
        return jnp.where(lane8 == nz - 1, 0.0, pltpu.roll(value, nz - 1, 1))

    def last_layer(value):
        return jnp.where(lane8 == 0, 0.0, pltpu.roll(value, 1, 1))

    dfull = total

    def build_diag():
        for x, y in columns:
            c = coef_pad[x + 1, y + 1]
            around = coef_pad[x, y + 1] + coef_pad[x + 2, y + 1] + coef_pad[x + 1, y] + coef_pad[x + 1, y + 2]
            around += next_layer(c) + last_layer(c)
            dfull[x, y] = spread(diag[x, y : y + 1]) + c * around

    build_diag()

    def operate(i):
        for x, y in columns:
            c = coef_pad[x + 1, y + 1]
            west, east = coef_pad[x, y + 1], coef_pad[x + 2, y + 1]
            south, north = coef_pad[x + 1, y], coef_pad[x + 1, y + 2]
            for h in range(kk // 8):
                ks = pl.ds(8 * h, 8)
                v = zs[i, x, y, ks]
                u = c * v
                near = next_layer(u) + last_layer(u)
                near += west * (zs[i, x - 1, y, ks] if x > 0 else halo_x[i, 0, y, ks])
                near += east * (zs[i, x + 1, y, ks] if x < cx - 1 else halo_x[i, 1, y, ks])
                near += south * (zs[i, x, y - 1, ks] if y > 0 else halo_y[i, 0, x, ks])
                near += north * (zs[i, x, y + 1, ks] if y < cy - 1 else halo_y[i, 1, x, ks])
                ws[i, x, y, ks] = dfull[x, y] * v - c * near

    def gram(lefts, rights):
        acc = None
        for x, y in columns:
            left_rows = jnp.concatenate([ref[x, y] for ref in lefts], axis=0)
            right_rows = jnp.concatenate([ref[x, y] for ref in rights], axis=0)
            product = dot_nt(left_rows, right_rows)
            acc = product if acc is None else acc + product
        return acc

    z_refs = [zs.at[i] for i in range(BASIS)]
    w_refs = [ws.at[i] for i in range(BASIS)]

    blocks = {}
    for i in range(BASIS):
        if i > 0:
            precondition(lambda x, y: ws[i - 1, x, y], store_z(i, BASIS_SCALE))
            flying = send_halo(i)
        known = gram([rhs] + w_refs[:i], [z_refs[i]])
        for r in range(i + 1):
            blocks[r, i] = known[kk * r : kk * (r + 1)]
        if i > 0:
            mirror = gram([z_refs[i]], w_refs[:i])
            for r in range(i):
                blocks[i + 1, r] = mirror[:, kk * r : kk * (r + 1)]
        for copy in flying:
            copy.wait()
        operate(i)
        own = gram([w_refs[i]], [z_refs[i]])
        blocks[i + 1, i] = own
    half = (BASIS + 1) * kk // 2
    span = BASIS * kk
    pad = jnp.zeros((half, 64 - span), F32)
    sums = jnp.concatenate(
        [jnp.concatenate([blocks[r, i] for r in range(BASIS + 1)], axis=0) for i in range(BASIS)], axis=1
    )
    sums = jnp.concatenate([sums[:half], pad, sums[half:], pad], axis=1)
    for r in range(half):
        part[r] = sums[r : r + 1]

    def start_all(axis, me, count, source, target, stage):
        @pl.loop(1, count)
        def _(d):
            peer = lax.rem(me + d, count)
            remote(source(peer), target(d), sum_send.at[stage], sum_recv.at[stage], {axis: peer}).start()

    def wait_all(buffer, count, stage, axis, peer):
        whole = buffer.at[pl.ds(0, count - 1)]
        done = remote(whole, whole, sum_send.at[stage], sum_recv.at[stage], {axis: peer})
        done.wait_send()
        done.wait_recv()

    start_all("wide", me_w, n_wide, lambda peer: part.at[peer], lambda d: rows_in.at[d - 1], 0)
    mine = part[me_w]
    wait_all(rows_in, n_wide, 0, "wide", right)
    for d in range(n_wide - 1):
        mine = mine + rows_in[d]
    plane[...] = mine
    start_all("narrow", me_n, n_narrow, lambda peer: plane, lambda d: plane_in.at[d - 1], 1)
    wait_all(plane_in, n_narrow, 1, "narrow", above)
    for d in range(n_narrow - 1):
        mine = mine + plane_in[d]
    all_rows[me_w] = mine
    start_all("wide", me_w, n_wide, lambda peer: all_rows.at[me_w], lambda d: all_rows.at[me_w], 2)
    wait_all(all_rows, n_wide, 2, "wide", right)

    packed = jnp.concatenate([all_rows[r] for r in range(half)], axis=0)
    low = packed
    high = pltpu.roll(packed, 64, 1)
    system = jnp.concatenate([low, high], axis=0)
    lanes = lax.broadcasted_iota(jnp.int32, (1, 128), 1)
    for k in range(span):
        pivot_row = system[kk + k : kk + k + 1]
        column = system[:, k : k + 1]
        factor = pivot_row / pivot_row[:, k : k + 1]
        inverse = 1.0 / pivot_row[:, k : k + 1]
        system = jnp.where(lanes == k, column * inverse, system - column * factor)
    y = system[:kk, :span]

    for x, yy in columns:
        basis = jnp.concatenate([zs[i, x, yy] for i in range(BASIS)], axis=0)
        image = jnp.concatenate([ws[i, x, yy] for i in range(BASIS)], axis=0)
        sol_ref[x, yy] = dot_nn(y, basis)
        res_ref[x, yy] = rhs[x, yy] - dot_nn(y, image)


def solution(mesh):
    n_wide, n_narrow = mesh.shape["wide"], mesh.shape["narrow"]

    def on_device(sources, well_columns, column_active, perm_root, storage_term, inverse_blocks):
        kk, cx, cy, nz = sources.shape
        nb, blk = inverse_blocks.shape[2], inverse_blocks.shape[3]
        rows = (BASIS + 1) * kk // 2
        field = jax.ShapeDtypeStruct((cx, cy, kk, nz), F32)
        dma = pltpu.SemaphoreType.DMA
        vmem = pltpu.VMEM
        out = pl.pallas_call(
            functools.partial(kernel, n_wide, n_narrow),
            out_shape=(field, field),
            in_specs=[pl.BlockSpec(memory_space=pl.ANY)] * 6,
            out_specs=(pl.BlockSpec(memory_space=vmem),) * 2,
            scratch_shapes=[
                vmem((cx, cy, kk, nz), F32),
                pltpu.SMEM(well_columns.shape, jnp.int32),
                pltpu.SMEM(column_active.shape, jnp.int32),
                vmem((cx, cy, nz), F32),
                vmem((cx, cy, nz), F32),
                vmem(inverse_blocks.shape, inverse_blocks.dtype),
                vmem((cx, cy, nz), F32),
                vmem((2, cx, cy, nz), F32),
                vmem((2, cy, nz), F32),
                vmem((cx + 2, cy + 2, 8, nz), F32),
                vmem((cx, cy, nz), F32),
                vmem((BASIS, cx, cy, kk, nz), F32),
                vmem((BASIS, cx, cy, kk, nz), F32),
                vmem((BASIS, 2, cy, kk, nz), F32),
                vmem((BASIS, 2, cx, kk, nz), F32),
                vmem((rows, 1, 128), F32),
                vmem((n_wide - 1, 1, 128), F32),
                vmem((n_narrow - 1, 1, 128), F32),
                vmem((1, 128), F32),
                vmem((rows, 1, 128), F32),
                vmem((cx, cy, 8, nz), F32),
                dma((5 + cx * cy,)),
                dma((4,)),
                dma((4,)),
                dma((BASIS, 4)),
                dma((BASIS, 4)),
                dma((3,)),
                dma((3,)),
            ],
            compiler_params=pltpu.CompilerParams(collective_id=0, has_side_effects=True),
        )(sources, well_columns, column_active, perm_root, storage_term, inverse_blocks)
        return tuple(jnp.transpose(value, (2, 0, 1, 3)) for value in out)

    in_specs = (
        P(None, "wide", "narrow", None),
        P(),
        P("wide", "narrow"),
        P("wide", "narrow", None),
        P("wide", "narrow", None),
        P("wide", "narrow", None, None, None),
    )
    out_specs = (P(None, "wide", "narrow", None), P(None, "wide", "narrow", None))
    return jax.shard_map(
        on_device, mesh=mesh, in_specs=in_specs, out_specs=out_specs, check_vma=False
    )
```

```python
import functools

import jax
import jax.numpy as jnp
from jax import lax
from jax.experimental import pallas as pl
from jax.experimental.pallas import tpu as pltpu
from jax.sharding import PartitionSpec as P

BASIS = 3
WELL_RATE = 4.0
BASIS_SCALE = 1.0 / 16.0
MESH = pl.DeviceIdType.MESH
EXACT = lax.Precision.HIGHEST
F32 = jnp.float32


def dot_nt(left, right):
    return lax.dot_general(left, right, (((1,), (1,)), ((), ())), precision=EXACT, preferred_element_type=F32)


def dot_nn(left, right):
    return lax.dot_general(left, right, (((1,), (0,)), ((), ())), precision=EXACT, preferred_element_type=F32)


def kernel(
    n_wide,
    n_narrow,
    src_hbm,
    wells_hbm,
    active_hbm,
    perm_hbm,
    storage_hbm,
    inv_hbm,
    sol_ref,
    res_ref,
    rhs,
    wells,
    active,
    perm,
    storage,
    inv,
    coef,
    coef_y,
    coef_x,
    coef_pad,
    diag,
    zs,
    ws,
    halo_x,
    halo_y,
    part,
    wide_in,
    plane,
    plane_in,
    part_c,
    wide_in_c,
    plane_c,
    plane_in_c,
    matrix,
    dfull,
    load_sem,
    coef_send,
    coef_recv,
    halo_send,
    halo_recv,
    sum_send,
    sum_recv,
):
    kk, cx, cy, nz = src_hbm.shape
    blk = inv_hbm.shape[-1]
    nb = inv_hbm.shape[2]
    me_w, me_n = lax.axis_index("wide"), lax.axis_index("narrow")
    right, left = lax.rem(me_w + 1, n_wide), lax.rem(me_w + n_wide - 1, n_wide)
    above, below = lax.rem(me_n + 1, n_narrow), lax.rem(me_n + n_narrow - 1, n_narrow)

    barrier = pltpu.get_barrier_semaphore()

    @pl.loop(1, n_narrow)
    def _(d):
        peer = lax.rem(me_n + d, n_narrow)
        pl.semaphore_signal(barrier, inc=1, device_id={"narrow": peer}, device_id_type=MESH)

    @pl.loop(1, n_wide)
    def _(d):
        peer = lax.rem(me_w + d, n_wide)
        pl.semaphore_signal(barrier, inc=1, device_id={"wide": peer}, device_id_type=MESH)

    loads = [
        pltpu.make_async_copy(wells_hbm, wells, load_sem.at[0]),
        pltpu.make_async_copy(active_hbm, active, load_sem.at[1]),
        pltpu.make_async_copy(perm_hbm, perm, load_sem.at[2]),
        pltpu.make_async_copy(storage_hbm, storage, load_sem.at[3]),
        pltpu.make_async_copy(inv_hbm, inv, load_sem.at[4]),
    ]
    columns = [(x, y) for x in range(cx) for y in range(cy)]
    for at, (x, y) in enumerate(columns):
        loads.append(pltpu.make_async_copy(src_hbm.at[:, x, y, :], rhs.at[x, y], load_sem.at[5 + at]))
    for load in loads:
        load.start()
    for load in loads[:4]:
        load.wait()

    row = lax.broadcasted_iota(jnp.int32, (cy, nz), 0)
    for x in range(cx):
        on = jnp.zeros((cy, nz), F32)
        for y in range(cy):
            on = jnp.where(row == y, active[x, y].astype(F32), on)
        coef[x] = perm[x] * on
        diag[x] = on * storage[x] + (1.0 - on)

    ids = lax.broadcasted_iota(jnp.int32, (kk, nz), 0)
    well_of = jnp.zeros((kk, nz), jnp.int32)
    for k in range(kk):
        well_of = jnp.where(ids == k, wells[k], well_of)
    for load in loads[4:]:
        load.wait()

    def precondition(source, i, x):
        for y in range(cy):
            value = source[x, y]
            high = value.astype(jnp.bfloat16)
            low = (value - high.astype(F32)).astype(jnp.bfloat16)
            both = jnp.concatenate([high, low], axis=0)
            for b in range(nb):
                out = lax.dot_general(
                    both[:, b * blk : (b + 1) * blk],
                    inv[x, y, b],
                    (((1,), (0,)), ((), ())),
                    preferred_element_type=F32,
                )
                out = out[:kk] + out[kk:]
                zs[i, x, y, :, b * blk : (b + 1) * blk] = out if i == 0 else out * BASIS_SCALE

    first_x, first_y = me_w * cx, me_n * cy
    for x, y in columns:
        here = (first_x + x) * (n_narrow * cy) + first_y + y
        rhs[x, y] = rhs[x, y] + jnp.where(well_of == here, WELL_RATE, 0.0)

    for x in range(cx):
        precondition(rhs, 0, x)

    pl.semaphore_wait(barrier, n_narrow + n_wide - 2)

    def remote(source, target, send, recv, device):
        return pltpu.make_async_remote_copy(
            src_ref=source, dst_ref=target, send_sem=send, recv_sem=recv, device_id=device, device_id_type=MESH
        )

    def halo_copies(i):
        return [
            remote(zs.at[i, cx - 1], halo_x.at[i, 0], halo_send.at[i, 0], halo_recv.at[i, 0], {"wide": right}),
            remote(zs.at[i, 0], halo_x.at[i, 1], halo_send.at[i, 1], halo_recv.at[i, 1], {"wide": left}),
            remote(zs.at[i, :, cy - 1], halo_y.at[i, 0], halo_send.at[i, 2], halo_recv.at[i, 2], {"narrow": above}),
            remote(zs.at[i, :, 0], halo_y.at[i, 1], halo_send.at[i, 3], halo_recv.at[i, 3], {"narrow": below}),
        ]

    coef_copies = [
        remote(coef.at[cx - 1], coef_x.at[0], coef_send.at[0], coef_recv.at[0], {"wide": right}),
        remote(coef.at[0], coef_x.at[1], coef_send.at[1], coef_recv.at[1], {"wide": left}),
        remote(coef, coef_y.at[0], coef_send.at[2], coef_recv.at[2], {"narrow": above}),
        remote(coef, coef_y.at[1], coef_send.at[3], coef_recv.at[3], {"narrow": below}),
    ]
    for copy in coef_copies:
        copy.start()
    flying = halo_copies(0)
    for copy in flying:
        copy.start()

    has_left = jnp.where(me_w == 0, 0.0, 1.0)
    has_right = jnp.where(me_w == n_wide - 1, 0.0, 1.0)
    has_below = jnp.where(me_n == 0, 0.0, 1.0)
    has_above = jnp.where(me_n == n_narrow - 1, 0.0, 1.0)

    def spread(line):
        return jnp.broadcast_to(line, (8, nz))

    for x, y in columns:
        coef_pad[x + 1, y + 1] = spread(coef[x, y : y + 1])
    for copy in coef_copies:
        copy.wait()
    for y in range(cy):
        coef_pad[0, y + 1] = spread(coef_x[0, y : y + 1] * has_left)
        coef_pad[cx + 1, y + 1] = spread(coef_x[1, y : y + 1] * has_right)
    for x in range(cx):
        coef_pad[x + 1, 0] = spread(coef_y[0, x, cy - 1 : cy] * has_below)
        coef_pad[x + 1, cy + 1] = spread(coef_y[1, x, 0:1] * has_above)

    lane8 = lax.broadcasted_iota(jnp.int32, (8, nz), 1)

    def next_layer(value):
        return jnp.where(lane8 == nz - 1, 0.0, pltpu.roll(value, nz - 1, 1))

    def last_layer(value):
        return jnp.where(lane8 == 0, 0.0, pltpu.roll(value, 1, 1))

    def build_diag():
        for x, y in columns:
            c = coef_pad[x + 1, y + 1]
            around = coef_pad[x, y + 1] + coef_pad[x + 2, y + 1] + coef_pad[x + 1, y] + coef_pad[x + 1, y + 2]
            around += next_layer(c) + last_layer(c)
            dfull[x, y] = spread(diag[x, y : y + 1]) + c * around

    build_diag()

    def operate_inside(i):
        for x, y in columns:
            c = coef_pad[x + 1, y + 1]
            for h in range(kk // 8):
                ks = pl.ds(8 * h, 8)
                v = zs[i, x, y, ks]
                u = c * v
                near = next_layer(u) + last_layer(u)
                if x > 0:
                    near += coef_pad[x, y + 1] * zs[i, x - 1, y, ks]
                if x < cx - 1:
                    near += coef_pad[x + 2, y + 1] * zs[i, x + 1, y, ks]
                if y > 0:
                    near += coef_pad[x + 1, y] * zs[i, x, y - 1, ks]
                if y < cy - 1:
                    near += coef_pad[x + 1, y + 2] * zs[i, x, y + 1, ks]
                ws[i, x, y, ks] = dfull[x, y] * v - c * near

    def operate_edge_y(i):
        for x in range(cx):
            for side, y, at in ((0, 0, 0), (1, cy - 1, cy + 1)):
                both = coef_pad[x + 1, y + 1] * coef_pad[x + 1, at]
                for h in range(kk // 8):
                    ks = pl.ds(8 * h, 8)
                    ws[i, x, y, ks] = ws[i, x, y, ks] - both * halo_y[i, side, x, ks]

    def operate_edge_x(i):
        for side, x, at in ((0, 0, 0), (1, cx - 1, cx + 1)):
            for y in range(cy):
                both = coef_pad[x + 1, y + 1] * coef_pad[at, y + 1]
                for h in range(kk // 8):
                    ks = pl.ds(8 * h, 8)
                    ws[i, x, y, ks] = ws[i, x, y, ks] - both * halo_x[i, side, y, ks]

    def gram(lefts, rights):
        acc = None
        for x, y in columns:
            left_rows = jnp.concatenate([ref[x, y] for ref in lefts], axis=0)
            right_rows = jnp.concatenate([ref[x, y] for ref in rights], axis=0)
            product = dot_nt(left_rows, right_rows)
            acc = product if acc is None else acc + product
        return acc

    def send_all(axis, me, count, source, target, send, recv):
        def send_to(d):
            peer = lax.rem(me + d, count)
            remote(source, target.at[d - 1], send, recv, {axis: peer}).start()

        send_to(count // 2)

        @pl.loop(1, count // 2)
        def _(t):
            send_to(count // 2 - t)
            send_to(count // 2 + t)

    def received(axis, peer, target, send, recv):
        done = remote(target, target, send, recv, {axis: peer})
        done.wait_recv()
        done.wait_send()

    def add_all(own, target):
        lines = [own] + [target[d] for d in range(target.shape[0])]
        while len(lines) > 1:
            lines = [a + b for a, b in zip(lines[::2], lines[1::2])] + lines[len(lines) // 2 * 2 :]
        return lines[0]

    sums = [(part, wide_in, plane, plane_in), (part, wide_in, plane, plane_in), (part_c, wide_in_c, plane_c, plane_in_c)]
    slot = [0, 1, 0]

    def sum_wide(j, value):
        own, into = sums[j][0].at[slot[j]], sums[j][1].at[slot[j]]
        own[...] = value
        send_all("wide", me_w, n_wide, own, into, sum_send.at[j, 0], sum_recv.at[j, 0])

    def sum_narrow(j):
        own, into, mid, last = (ref.at[slot[j]] for ref in sums[j])
        received("wide", right, into, sum_send.at[j, 0], sum_recv.at[j, 0])
        mid[...] = add_all(own[...], into)
        send_all("narrow", me_n, n_narrow, mid, last, sum_send.at[j, 1], sum_recv.at[j, 1])

    def sum_done(j):
        mid, last = sums[j][2].at[slot[j]], sums[j][3].at[slot[j]]
        received("narrow", above, last, sum_send.at[j, 1], sum_recv.at[j, 1])
        return add_all(mid[...], last)

    z_refs = [zs.at[i] for i in range(BASIS)]
    w_refs = [ws.at[i] for i in range(BASIS)]

    def halve(line):
        return jnp.concatenate([line[:8], line[8:]], axis=1)

    for i in range(BASIS):
        if i > 0:
            flying = halo_copies(i)
            for x in reversed(range(cx)):
                precondition(w_refs[i - 1], i, x)
                if x == cx - 1:
                    flying[0].start()
                if x == 0:
                    flying[1].start()
            flying[2].start()
            flying[3].start()
        operate_inside(i)
        if i == 1:
            first = gram([rhs, w_refs[0]], [z_refs[0], z_refs[1]])
            sum_wide(0, halve(jnp.concatenate([first[:kk], first[kk:]], axis=1)))
        if i == 2:
            second = gram([rhs, w_refs[0], w_refs[1]], [z_refs[1], z_refs[2]])
            line = [second[:kk, kk:], second[kk : 2 * kk, kk:], second[2 * kk :]]
            sum_wide(1, halve(jnp.concatenate(line, axis=1)))
            sum_narrow(0)
        for copy in flying[2:]:
            copy.wait()
        operate_edge_y(i)
        for copy in flying[:2]:
            copy.wait()
        operate_edge_x(i)

    lanes = lax.broadcasted_iota(jnp.int32, (kk, 128), 1)
    rows = lax.broadcasted_iota(jnp.int32, (kk, 128), 0)
    diagonal = lanes // kk == lax.rem(rows, 8)
    third = gram([w_refs[2]], [z_refs[2]])
    third = jnp.where(diagonal, jnp.concatenate([third] * 8, axis=1), 0.0)
    sum_wide(2, jnp.concatenate([jnp.sum(third[:8], axis=0, keepdims=True), jnp.sum(third[8:], axis=0, keepdims=True)], axis=0))

    matrix[...] = jnp.zeros_like(matrix)
    sum_narrow(1)
    first = sum_done(0)
    for h in range(2):
        matrix[8 * h : 8 * h + 8, 0 : 2 * kk] = first[:, 64 * h : 64 * h + 2 * kk]
        matrix[kk + 8 * h : kk + 8 * h + 8, 0 : 2 * kk] = first[:, 64 * h + 2 * kk : 64 * h + 4 * kk]
    sum_narrow(2)
    second = sum_done(1)
    for h in range(2):
        for r in range(2):
            piece = second[:, 64 * h + r * kk : 64 * h + (r + 1) * kk]
            matrix[r * kk + 8 * h : r * kk + 8 * h + 8, 2 * kk : 3 * kk] = piece
        matrix[2 * kk + 8 * h : 2 * kk + 8 * h + 8, kk : 3 * kk] = second[:, 64 * h + 2 * kk : 64 * h + 4 * kk]
    pick_rows = lax.broadcasted_iota(jnp.int32, (2 * kk, 128), 0)
    pick_lanes = lax.broadcasted_iota(jnp.int32, (2 * kk, 128), 1)
    pick = jnp.where(pick_lanes == pick_rows + kk, 1.0, 0.0)
    matrix[2 * kk :, 0 : 2 * kk] = dot_nt(pick, matrix[kk : 3 * kk])

    lane = lax.broadcasted_iota(jnp.int32, (1, 128), 1)

    def eliminate(system, row, k):
        shape = system.shape
        c0 = jnp.broadcast_to(system[:, k : k + 1], shape)
        c1 = jnp.broadcast_to(system[:, k + 1 : k + 2], shape)
        p0, p1 = system[row : row + 1], system[row + 1 : row + 2]
        a, b = c0[row : row + 1], c1[row : row + 1]
        c, d = c0[row + 1 : row + 2], c1[row + 1 : row + 2]
        inverse = 1.0 / (a * d - b * c)
        at0, at1 = lane == k, lane == k + 1
        g0 = jnp.where(at0, -d, jnp.where(at1, b, d * p0 - b * p1)) * inverse
        g1 = jnp.where(at0, c, jnp.where(at1, -a, a * p1 - c * p0)) * inverse
        kept = jnp.where(at0 | at1, 0.0, system)
        return kept - c0 * g0 - c1 * g1

    system = matrix[...]
    for k in range(0, 2 * kk, 2):
        system = eliminate(system, kk + k, k)

    third = sum_done(2)
    third = jnp.concatenate([jnp.broadcast_to(third[h : h + 1], (8, 128)) for h in range(2)], axis=0)
    third = jnp.where(diagonal, third, 0.0)
    for shift in (64, 32, 16):
        third = third + pltpu.roll(third, shift, 1)
    third = jnp.where((lanes >= 2 * kk) & (lanes < 3 * kk), third, 0.0)
    system = jnp.concatenate([system[:kk], system[3 * kk :] + third], axis=0)
    for k in range(0, kk, 2):
        system = eliminate(system, kk + k, 2 * kk + k)
    y = system[:kk, : BASIS * kk]

    for x, yy in columns:
        basis = jnp.concatenate([zs[i, x, yy] for i in range(BASIS)], axis=0)
        image = jnp.concatenate([ws[i, x, yy] for i in range(BASIS)], axis=0)
        sol_ref[x, yy] = dot_nn(y, basis)
        res_ref[x, yy] = rhs[x, yy] - dot_nn(y, image)


def solution(mesh):
    n_wide, n_narrow = mesh.shape["wide"], mesh.shape["narrow"]

    def on_device(sources, well_columns, column_active, perm_root, storage_term, inverse_blocks):
        kk, cx, cy, nz = sources.shape
        nb, blk = inverse_blocks.shape[2], inverse_blocks.shape[3]
        field = jax.ShapeDtypeStruct((cx, cy, kk, nz), F32)
        dma = pltpu.SemaphoreType.DMA
        vmem = pltpu.VMEM
        out = pl.pallas_call(
            functools.partial(kernel, n_wide, n_narrow),
            out_shape=(field, field),
            in_specs=[pl.BlockSpec(memory_space=pl.ANY)] * 6,
            out_specs=(pl.BlockSpec(memory_space=vmem),) * 2,
            scratch_shapes=[
                vmem((cx, cy, kk, nz), F32),
                pltpu.SMEM(well_columns.shape, jnp.int32),
                pltpu.SMEM(column_active.shape, jnp.int32),
                vmem((cx, cy, nz), F32),
                vmem((cx, cy, nz), F32),
                vmem(inverse_blocks.shape, inverse_blocks.dtype),
                vmem((cx, cy, nz), F32),
                vmem((2, cx, cy, nz), F32),
                vmem((2, cy, nz), F32),
                vmem((cx + 2, cy + 2, 8, nz), F32),
                vmem((cx, cy, nz), F32),
                vmem((BASIS, cx, cy, kk, nz), F32),
                vmem((BASIS, cx, cy, kk, nz), F32),
                vmem((BASIS, 2, cy, kk, nz), F32),
                vmem((BASIS, 2, cx, kk, nz), F32),
                vmem((2, 8, 128), F32),
                vmem((2, n_wide - 1, 8, 128), F32),
                vmem((2, 8, 128), F32),
                vmem((2, n_narrow - 1, 8, 128), F32),
                vmem((1, 2, 128), F32),
                vmem((1, n_wide - 1, 2, 128), F32),
                vmem((1, 2, 128), F32),
                vmem((1, n_narrow - 1, 2, 128), F32),
                vmem(((BASIS + 1) * kk, 128), F32),
                vmem((cx, cy, 8, nz), F32),
                dma((5 + cx * cy,)),
                dma((4,)),
                dma((4,)),
                dma((BASIS, 4)),
                dma((BASIS, 4)),
                dma((3, 2)),
                dma((3, 2)),
            ],
            compiler_params=pltpu.CompilerParams(collective_id=0, has_side_effects=True),
        )(sources, well_columns, column_active, perm_root, storage_term, inverse_blocks)
        return tuple(jnp.transpose(value, (2, 0, 1, 3)) for value in out)

    in_specs = (
        P(None, "wide", "narrow", None),
        P(),
        P("wide", "narrow"),
        P("wide", "narrow", None),
        P("wide", "narrow", None),
        P("wide", "narrow", None, None, None),
    )
    out_specs = (P(None, "wide", "narrow", None), P(None, "wide", "narrow", None))
    return jax.shard_map(
        on_device, mesh=mesh, in_specs=in_specs, out_specs=out_specs, check_vma=False
    )
```

```python
import functools

import jax
import jax.numpy as jnp
from jax import lax
from jax.experimental import pallas as pl
from jax.experimental.pallas import tpu as pltpu
from jax.sharding import PartitionSpec as P

BASIS = 3
WELL_RATE = 4.0
BASIS_SCALE = 1.0 / 16.0
MESH = pl.DeviceIdType.MESH
EXACT = lax.Precision.HIGHEST
SPLIT = lax.Precision.HIGH
CHUNKS = 4
F32 = jnp.float32


def dot_nt(left, right, precision=EXACT):
    return lax.dot_general(left, right, (((1,), (1,)), ((), ())), precision=precision, preferred_element_type=F32)


def dot_nn(left, right):
    return lax.dot_general(left, right, (((1,), (0,)), ((), ())), precision=SPLIT, preferred_element_type=F32)


def kernel(
    n_wide,
    n_narrow,
    src_hbm,
    wells_hbm,
    active_hbm,
    perm_hbm,
    storage_hbm,
    inv_hbm,
    weights,
    rhs,
    zs,
    ws,
    wells,
    active,
    perm,
    storage,
    inv,
    coef,
    coef_y,
    coef_x,
    coef_pad,
    diag,
    halo_x,
    halo_y,
    part,
    wide_in,
    plane,
    plane_in,
    part_c,
    wide_in_c,
    plane_c,
    plane_in_c,
    matrix,
    dfull,
    load_sem,
    coef_send,
    coef_recv,
    halo_send,
    halo_recv,
    sum_send,
    sum_recv,
):
    kk, cx, cy, nz = src_hbm.shape
    blk = inv_hbm.shape[-1]
    nb = inv_hbm.shape[2]
    me_w, me_n = lax.axis_index("wide"), lax.axis_index("narrow")
    right, left = lax.rem(me_w + 1, n_wide), lax.rem(me_w + n_wide - 1, n_wide)
    above, below = lax.rem(me_n + 1, n_narrow), lax.rem(me_n + n_narrow - 1, n_narrow)

    barrier = pltpu.get_barrier_semaphore()

    @pl.loop(1, n_narrow)
    def _(d):
        peer = lax.rem(me_n + d, n_narrow)
        pl.semaphore_signal(barrier, inc=1, device_id={"narrow": peer}, device_id_type=MESH)

    @pl.loop(1, n_wide)
    def _(d):
        peer = lax.rem(me_w + d, n_wide)
        pl.semaphore_signal(barrier, inc=1, device_id={"wide": peer}, device_id_type=MESH)

    loads = [
        pltpu.make_async_copy(wells_hbm, wells, load_sem.at[0]),
        pltpu.make_async_copy(active_hbm, active, load_sem.at[1]),
        pltpu.make_async_copy(perm_hbm, perm, load_sem.at[2]),
        pltpu.make_async_copy(storage_hbm, storage, load_sem.at[3]),
        pltpu.make_async_copy(inv_hbm, inv, load_sem.at[4]),
    ]
    columns = [(x, y) for x in range(cx) for y in range(cy)]
    for at, (x, y) in enumerate(columns):
        loads.append(pltpu.make_async_copy(src_hbm.at[:, x, y, :], rhs.at[x, y], load_sem.at[5 + at]))
    for load in loads:
        load.start()
    for load in loads[:4]:
        load.wait()

    row = lax.broadcasted_iota(jnp.int32, (cy, nz), 0)
    for x in range(cx):
        on = jnp.zeros((cy, nz), F32)
        for y in range(cy):
            on = jnp.where(row == y, active[x, y].astype(F32), on)
        coef[x] = perm[x] * on
        diag[x] = on * storage[x] + (1.0 - on)

    ids = lax.broadcasted_iota(jnp.int32, (kk, nz), 0)
    well_of = jnp.zeros((kk, nz), jnp.int32)
    for k in range(kk):
        well_of = jnp.where(ids == k, wells[k], well_of)
    for load in loads[4:]:
        load.wait()

    wide_y = cy // CHUNKS
    order = [0, CHUNKS - 1] + list(range(1, CHUNKS - 1))

    def chunk(c):
        return [(x, y) for x in reversed(range(cx)) for y in range(c * wide_y, (c + 1) * wide_y)]

    def precondition(source, i, c):
        for x, y in chunk(c):
            value = source[x, y]
            high = value.astype(jnp.bfloat16)
            low = (value - high.astype(F32)).astype(jnp.bfloat16)
            both = jnp.concatenate([high, low], axis=0)
            for b in range(nb):
                out = lax.dot_general(
                    both[:, b * blk : (b + 1) * blk],
                    inv[x, y, b],
                    (((1,), (0,)), ((), ())),
                    preferred_element_type=F32,
                )
                out = out[:kk] + out[kk:]
                zs[i, x, y, :, b * blk : (b + 1) * blk] = out if i == 0 else out * BASIS_SCALE

    first_x, first_y = me_w * cx, me_n * cy
    for x, y in columns:
        here = (first_x + x) * (n_narrow * cy) + first_y + y
        rhs[x, y] = rhs[x, y] + jnp.where(well_of == here, WELL_RATE, 0.0)

    for c in order:
        precondition(rhs, 0, c)

    pl.semaphore_wait(barrier, n_narrow + n_wide - 2)

    def remote(source, target, send, recv, device):
        return pltpu.make_async_remote_copy(
            src_ref=source, dst_ref=target, send_sem=send, recv_sem=recv, device_id=device, device_id_type=MESH
        )

    def copy_x(i, side, c):
        ys = pl.ds(c * wide_y, wide_y)
        source, device = ((cx - 1, {"wide": right}), (0, {"wide": left}))[side]
        send, recv = halo_send.at[i, 2 + 2 * c + side], halo_recv.at[i, 2 + 2 * c + side]
        return remote(zs.at[i, source, ys], halo_x.at[i, side, ys], send, recv, device)

    def copy_y(i, side):
        source, device = ((cy - 1, {"narrow": above}), (0, {"narrow": below}))[side]
        return remote(zs.at[i, :, source], halo_y.at[i, side], halo_send.at[i, side], halo_recv.at[i, side], device)

    def emit(i, c):
        copy_x(i, 0, c).start()
        copy_x(i, 1, c).start()
        if c == CHUNKS - 1:
            copy_y(i, 0).start()
        if c == 0:
            copy_y(i, 1).start()

    coef_copies = [
        remote(coef.at[cx - 1], coef_x.at[0], coef_send.at[0], coef_recv.at[0], {"wide": right}),
        remote(coef.at[0], coef_x.at[1], coef_send.at[1], coef_recv.at[1], {"wide": left}),
        remote(coef, coef_y.at[0], coef_send.at[2], coef_recv.at[2], {"narrow": above}),
        remote(coef, coef_y.at[1], coef_send.at[3], coef_recv.at[3], {"narrow": below}),
    ]
    for copy in coef_copies:
        copy.start()
    for c in order:
        emit(0, c)

    has_left = jnp.where(me_w == 0, 0.0, 1.0)
    has_right = jnp.where(me_w == n_wide - 1, 0.0, 1.0)
    has_below = jnp.where(me_n == 0, 0.0, 1.0)
    has_above = jnp.where(me_n == n_narrow - 1, 0.0, 1.0)

    def spread(line):
        return jnp.broadcast_to(line, (8, nz))

    for x, y in columns:
        coef_pad[x + 1, y + 1] = spread(coef[x, y : y + 1])
    lane8 = lax.broadcasted_iota(jnp.int32, (8, nz), 1)

    def next_layer(value):
        return jnp.where(lane8 == nz - 1, 0.0, pltpu.roll(value, nz - 1, 1))

    def last_layer(value):
        return jnp.where(lane8 == 0, 0.0, pltpu.roll(value, 1, 1))

    def coupled(x, y):
        if x > 0:
            yield (x, y + 1), (x - 1, y)
        if x < cx - 1:
            yield (x + 2, y + 1), (x + 1, y)
        if y > 0:
            yield (x + 1, y), (x, y - 1)
        if y < cy - 1:
            yield (x + 1, y + 2), (x, y + 1)

    for x, y in columns:
        c = coef_pad[x + 1, y + 1]
        around = next_layer(c) + last_layer(c)
        for at, _ in coupled(x, y):
            around += coef_pad[at]
        dfull[x, y] = spread(diag[x, y : y + 1]) + c * around

    def operate_inside(i):
        for x, y in columns:
            c = coef_pad[x + 1, y + 1]
            for h in range(kk // 8):
                ks = pl.ds(8 * h, 8)
                v = zs[i, x, y, ks]
                u = c * v
                near = next_layer(u) + last_layer(u)
                for at, (nx, ny) in coupled(x, y):
                    near += coef_pad[at] * zs[i, nx, ny, ks]
                ws[i, x, y, ks] = dfull[x, y] * v - c * near

    def absorb(i, c):
        copy_x(i, 0, c).wait()
        copy_x(i, 1, c).wait()
        if c == 0:
            copy_y(i, 0).wait()
        if c == CHUNKS - 1:
            copy_y(i, 1).wait()
        for x, y in chunk(c):
            edges = []
            if x == 0:
                edges.append(((0, y + 1), halo_x.at[i, 0, y]))
            if x == cx - 1:
                edges.append(((cx + 1, y + 1), halo_x.at[i, 1, y]))
            if y == 0:
                edges.append(((x + 1, 0), halo_y.at[i, 0, x]))
            if y == cy - 1:
                edges.append(((x + 1, cy + 1), halo_y.at[i, 1, x]))
            both = [coef_pad[x + 1, y + 1] * coef_pad[at] for at, _ in edges]
            for h in range(kk // 8):
                ks = pl.ds(8 * h, 8)
                v, w = zs[i, x, y, ks], ws[i, x, y, ks]
                for pair, (_, outer) in zip(both, edges):
                    w += pair * (v - outer[ks])
                ws[i, x, y, ks] = w

    def gram(lefts, rights):
        acc = None
        for x, y in columns:
            left_rows = jnp.concatenate([ref[x, y] for ref in lefts], axis=0)
            right_rows = jnp.concatenate([ref[x, y] for ref in rights], axis=0)
            product = dot_nt(left_rows, right_rows, SPLIT)
            acc = product if acc is None else acc + product
        return acc

    def send_all(axis, me, count, source, target, send, recv):
        def send_to(d):
            peer = lax.rem(me + d, count)
            remote(source, target.at[d - 1], send, recv, {axis: peer}).start()

        send_to(count // 2)

        @pl.loop(1, count // 2)
        def _(t):
            send_to(count // 2 - t)
            send_to(count // 2 + t)

    def received(axis, peer, target, send, recv):
        done = remote(target, target, send, recv, {axis: peer})
        done.wait_recv()
        done.wait_send()

    def add_all(own, target):
        lines = [own] + [target[d] for d in range(target.shape[0])]
        while len(lines) > 1:
            lines = [a + b for a, b in zip(lines[::2], lines[1::2])] + lines[len(lines) // 2 * 2 :]
        return lines[0]

    sums = [(part, wide_in, plane, plane_in), (part, wide_in, plane, plane_in), (part_c, wide_in_c, plane_c, plane_in_c)]
    slot = [0, 1, 0]

    def sum_wide(j, value):
        own, into = sums[j][0].at[slot[j]], sums[j][1].at[slot[j]]
        own[...] = value
        send_all("wide", me_w, n_wide, own, into, sum_send.at[j, 0], sum_recv.at[j, 0])

    def sum_narrow(j):
        own, into, mid, last = (ref.at[slot[j]] for ref in sums[j])
        received("wide", right, into, sum_send.at[j, 0], sum_recv.at[j, 0])
        mid[...] = add_all(own[...], into)
        send_all("narrow", me_n, n_narrow, mid, last, sum_send.at[j, 1], sum_recv.at[j, 1])

    def sum_done(j):
        mid, last = sums[j][2].at[slot[j]], sums[j][3].at[slot[j]]
        received("narrow", above, last, sum_send.at[j, 1], sum_recv.at[j, 1])
        return add_all(mid[...], last)

    z_refs = [zs.at[i] for i in range(BASIS)]
    w_refs = [ws.at[i] for i in range(BASIS)]

    def halve(line):
        return jnp.concatenate([line[:8], line[8:]], axis=1)

    for i in range(BASIS):
        if i > 0:
            for c in order:
                absorb(i - 1, c)
                precondition(w_refs[i - 1], i, c)
                emit(i, c)
        operate_inside(i)
        if i == 0:
            for copy in coef_copies:
                copy.wait()
            for y in range(cy):
                coef_pad[0, y + 1] = spread(coef_x[0, y : y + 1] * has_left)
                coef_pad[cx + 1, y + 1] = spread(coef_x[1, y : y + 1] * has_right)
            for x in range(cx):
                coef_pad[x + 1, 0] = spread(coef_y[0, x, cy - 1 : cy] * has_below)
                coef_pad[x + 1, cy + 1] = spread(coef_y[1, x, 0:1] * has_above)
        if i == 1:
            first = gram([rhs, w_refs[0]], [z_refs[0], z_refs[1]])
            sum_wide(0, halve(jnp.concatenate([first[:kk], first[kk:]], axis=1)))
        if i == 2:
            second = gram([rhs, w_refs[0], w_refs[1]], [z_refs[1], z_refs[2]])
            line = [second[:kk, kk:], second[kk : 2 * kk, kk:], second[2 * kk :]]
            sum_wide(1, halve(jnp.concatenate(line, axis=1)))
            sum_narrow(0)
    for c in order:
        absorb(BASIS - 1, c)

    lanes = lax.broadcasted_iota(jnp.int32, (kk, 128), 1)
    rows = lax.broadcasted_iota(jnp.int32, (kk, 128), 0)
    diagonal = lanes // kk == lax.rem(rows, 8)
    third = gram([w_refs[2]], [z_refs[2]])
    third = jnp.where(diagonal, jnp.concatenate([third] * 8, axis=1), 0.0)
    sum_wide(2, jnp.concatenate([jnp.sum(third[:8], axis=0, keepdims=True), jnp.sum(third[8:], axis=0, keepdims=True)], axis=0))

    matrix[...] = jnp.zeros_like(matrix)
    sum_narrow(1)
    first = sum_done(0)
    for h in range(2):
        matrix[8 * h : 8 * h + 8, 0 : 2 * kk] = first[:, 64 * h : 64 * h + 2 * kk]
        matrix[kk + 8 * h : kk + 8 * h + 8, 0 : 2 * kk] = first[:, 64 * h + 2 * kk : 64 * h + 4 * kk]
    sum_narrow(2)
    second = sum_done(1)
    for h in range(2):
        for r in range(2):
            piece = second[:, 64 * h + r * kk : 64 * h + (r + 1) * kk]
            matrix[r * kk + 8 * h : r * kk + 8 * h + 8, 2 * kk : 3 * kk] = piece
        matrix[2 * kk + 8 * h : 2 * kk + 8 * h + 8, kk : 3 * kk] = second[:, 64 * h + 2 * kk : 64 * h + 4 * kk]
    pick_rows = lax.broadcasted_iota(jnp.int32, (2 * kk, 128), 0)
    pick_lanes = lax.broadcasted_iota(jnp.int32, (2 * kk, 128), 1)
    pick = jnp.where(pick_lanes == pick_rows + kk, 1.0, 0.0)
    matrix[2 * kk :, 0 : 2 * kk] = dot_nt(pick, matrix[kk : 3 * kk])

    lane = lax.broadcasted_iota(jnp.int32, (1, 128), 1)

    def eliminate(system, row, k):
        shape = system.shape
        c0 = jnp.broadcast_to(system[:, k : k + 1], shape)
        c1 = jnp.broadcast_to(system[:, k + 1 : k + 2], shape)
        p0, p1 = system[row : row + 1], system[row + 1 : row + 2]
        a, b = c0[row : row + 1], c1[row : row + 1]
        c, d = c0[row + 1 : row + 2], c1[row + 1 : row + 2]
        inverse = 1.0 / (a * d - b * c)
        at0, at1 = lane == k, lane == k + 1
        g0 = jnp.where(at0, -d, jnp.where(at1, b, d * p0 - b * p1)) * inverse
        g1 = jnp.where(at0, c, jnp.where(at1, -a, a * p1 - c * p0)) * inverse
        kept = jnp.where(at0 | at1, 0.0, system)
        return kept - c0 * g0 - c1 * g1

    system = matrix[...]
    for k in range(0, 2 * kk, 2):
        system = eliminate(system, kk + k, k)

    third = sum_done(2)
    third = jnp.concatenate([jnp.broadcast_to(third[h : h + 1], (8, 128)) for h in range(2)], axis=0)
    third = jnp.where(diagonal, third, 0.0)
    for shift in (64, 32, 16):
        third = third + pltpu.roll(third, shift, 1)
    third = jnp.where((lanes >= 2 * kk) & (lanes < 3 * kk), third, 0.0)
    system = jnp.concatenate([system[:kk], system[3 * kk :] + third], axis=0)
    for k in range(0, kk, 2):
        system = eliminate(system, kk + k, 2 * kk + k)
    weights[...] = system[:kk]


def combine(weights, rhs, zs, ws, sol_hbm, res_hbm, sol, res, out_sem):
    cx, cy, kk, nz = rhs.shape
    y = weights[:, : BASIS * kk]
    copies = []
    for x in range(cx):
        for yy in range(cy):
            basis = jnp.concatenate([zs[i, x, yy] for i in range(BASIS)], axis=0)
            image = jnp.concatenate([ws[i, x, yy] for i in range(BASIS)], axis=0)
            sol[x, yy] = dot_nn(y, basis)
            res[x, yy] = rhs[x, yy] - dot_nn(y, image)
            for buffer, target in ((sol, sol_hbm), (res, res_hbm)):
                copy = pltpu.make_async_copy(buffer.at[x, yy], target.at[:, x, yy, :], out_sem.at[len(copies)])
                copy.start()
                copies.append(copy)
    for copy in copies:
        copy.wait()


def solution(mesh):
    n_wide, n_narrow = mesh.shape["wide"], mesh.shape["narrow"]

    def on_device(sources, well_columns, column_active, perm_root, storage_term, inverse_blocks):
        kk, cx, cy, nz = sources.shape
        nb, blk = inverse_blocks.shape[2], inverse_blocks.shape[3]
        dma = pltpu.SemaphoreType.DMA
        vmem = pltpu.VMEM
        held = pl.pallas_call(
            functools.partial(kernel, n_wide, n_narrow),
            out_shape=(
                vmem((kk, 128), F32),
                vmem((cx, cy, kk, nz), F32),
                vmem((BASIS, cx, cy, kk, nz), F32),
                vmem((BASIS, cx, cy, kk, nz), F32),
            ),
            in_specs=[pl.BlockSpec(memory_space=pl.ANY)] * 6,
            out_specs=(pl.BlockSpec(memory_space=vmem),) * 4,
            scratch_shapes=[
                pltpu.SMEM(well_columns.shape, jnp.int32),
                pltpu.SMEM(column_active.shape, jnp.int32),
                vmem((cx, cy, nz), F32),
                vmem((cx, cy, nz), F32),
                vmem(inverse_blocks.shape, inverse_blocks.dtype),
                vmem((cx, cy, nz), F32),
                vmem((2, cx, cy, nz), F32),
                vmem((2, cy, nz), F32),
                vmem((cx + 2, cy + 2, 8, nz), F32),
                vmem((cx, cy, nz), F32),
                vmem((BASIS, 2, cy, kk, nz), F32),
                vmem((BASIS, 2, cx, kk, nz), F32),
                vmem((2, 8, 128), F32),
                vmem((2, n_wide - 1, 8, 128), F32),
                vmem((2, 8, 128), F32),
                vmem((2, n_narrow - 1, 8, 128), F32),
                vmem((1, 2, 128), F32),
                vmem((1, n_wide - 1, 2, 128), F32),
                vmem((1, 2, 128), F32),
                vmem((1, n_narrow - 1, 2, 128), F32),
                vmem(((BASIS + 1) * kk, 128), F32),
                vmem((cx, cy, 8, nz), F32),
                dma((5 + cx * cy,)),
                dma((4,)),
                dma((4,)),
                dma((BASIS, 2 + 2 * CHUNKS)),
                dma((BASIS, 2 + 2 * CHUNKS)),
                dma((3, 2)),
                dma((3, 2)),
            ],
            compiler_params=pltpu.CompilerParams(collective_id=0, has_side_effects=True),
        )(sources, well_columns, column_active, perm_root, storage_term, inverse_blocks)
        field = jax.ShapeDtypeStruct(sources.shape, F32)
        return pl.pallas_call(
            combine,
            out_shape=(field, field),
            in_specs=[pl.BlockSpec(memory_space=vmem)] * 4,
            out_specs=(pl.BlockSpec(memory_space=pl.ANY),) * 2,
            scratch_shapes=[
                vmem((cx, cy, kk, nz), F32),
                vmem((cx, cy, kk, nz), F32),
                dma((2 * cx * cy,)),
            ],
        )(*(pltpu.with_memory_space_constraint(value, vmem) for value in held))

    in_specs = (
        P(None, "wide", "narrow", None),
        P(),
        P("wide", "narrow"),
        P("wide", "narrow", None),
        P("wide", "narrow", None),
        P("wide", "narrow", None, None, None),
    )
    out_specs = (P(None, "wide", "narrow", None), P(None, "wide", "narrow", None))
    return jax.shard_map(
        on_device, mesh=mesh, in_specs=in_specs, out_specs=out_specs, check_vma=False
    )
```

```python
import functools

import jax
import jax.numpy as jnp
from jax import lax
from jax.experimental import pallas as pl
from jax.experimental.pallas import tpu as pltpu
from jax.sharding import PartitionSpec as P

BASIS = 3
WELL_RATE = 4.0
BASIS_SCALE = 1.0 / 16.0
MESH = pl.DeviceIdType.MESH
EXACT = lax.Precision.HIGHEST
SPLIT = lax.Precision.HIGH
CHUNKS = 4
F32 = jnp.float32


def dot_nt(left, right, precision=EXACT):
    return lax.dot_general(left, right, (((1,), (1,)), ((), ())), precision=precision, preferred_element_type=F32)


def dot_nn(left, right):
    return lax.dot_general(left, right, (((1,), (0,)), ((), ())), precision=SPLIT, preferred_element_type=F32)


def kernel(
    n_wide,
    n_narrow,
    src_hbm,
    wells_hbm,
    active_hbm,
    perm_hbm,
    storage_hbm,
    inv_hbm,
    weights,
    rhs,
    zs,
    ws,
    wells,
    active,
    perm,
    storage,
    inv,
    coef,
    coef_y,
    coef_x,
    coef_pad,
    diag,
    halo_x,
    halo_y,
    part,
    wide_in,
    plane,
    plane_in,
    part_c,
    wide_in_c,
    plane_c,
    plane_in_c,
    matrix,
    dfull,
    load_sem,
    coef_send,
    coef_recv,
    halo_send,
    halo_recv,
    sum_send,
    sum_recv,
    tokens,
):
    kk, cx, cy, nz = src_hbm.shape
    blk = inv_hbm.shape[-1]
    nb = inv_hbm.shape[2]
    me_w, me_n = lax.axis_index("wide"), lax.axis_index("narrow")
    right, left = lax.rem(me_w + 1, n_wide), lax.rem(me_w + n_wide - 1, n_wide)
    above, below = lax.rem(me_n + 1, n_narrow), lax.rem(me_n + n_narrow - 1, n_narrow)

    barrier = pltpu.get_barrier_semaphore()

    for axis, peer in (("wide", right), ("wide", left), ("narrow", above), ("narrow", below)):
        pl.semaphore_signal(barrier, inc=1, device_id={axis: peer}, device_id_type=MESH)

    rings = {"wide": (0, me_w, n_wide), "narrow": (1, me_n, n_narrow)}

    def tell(axis, r):
        at, me, count = rings[axis]
        for d in (2**r, count - 2**r):
            peer = lax.rem(me + d, count)
            pl.semaphore_signal(tokens.at[at, r], inc=1, device_id={axis: peer}, device_id_type=MESH)

    def hear(axis, r):
        pl.semaphore_wait(tokens.at[rings[axis][0], r], 2)

    loads = [
        pltpu.make_async_copy(wells_hbm, wells, load_sem.at[0]),
        pltpu.make_async_copy(active_hbm, active, load_sem.at[1]),
        pltpu.make_async_copy(perm_hbm, perm, load_sem.at[2]),
        pltpu.make_async_copy(storage_hbm, storage, load_sem.at[3]),
    ]
    wide_y = cy // CHUNKS
    order = [0, CHUNKS - 1] + list(range(1, CHUNKS - 1))

    def chunk(c):
        return [(x, y) for x in reversed(range(cx)) for y in range(c * wide_y, (c + 1) * wide_y)]

    columns = [(x, y) for x in range(cx) for y in range(cy)]
    chunk_loads = {}
    for c in order:
        ys = pl.ds(c * wide_y, wide_y)
        own = [(inv_hbm.at[x, ys], inv.at[x, ys]) for x in range(cx)]
        own += [(src_hbm.at[:, x, y, :], rhs.at[x, y]) for x, y in chunk(c)]
        first = 4 + c * len(own)
        chunk_loads[c] = [
            pltpu.make_async_copy(source, target, load_sem.at[first + at]) for at, (source, target) in enumerate(own)
        ]
    for load in loads + [load for c in order for load in chunk_loads[c]]:
        load.start()
    pl.semaphore_wait(barrier, 4)
    tell("wide", 0)
    tell("narrow", 0)
    for load in loads:
        load.wait()

    row = lax.broadcasted_iota(jnp.int32, (cy, nz), 0)
    for x in range(cx):
        on = jnp.zeros((cy, nz), F32)
        for y in range(cy):
            on = jnp.where(row == y, active[x, y].astype(F32), on)
        coef[x] = perm[x] * on
        diag[x] = on * storage[x] + (1.0 - on)

    ids = lax.broadcasted_iota(jnp.int32, (kk, nz), 0)
    well_of = jnp.zeros((kk, nz), jnp.int32)
    for k in range(kk):
        well_of = jnp.where(ids == k, wells[k], well_of)

    def precondition(source, i, c):
        for x, y in chunk(c):
            value = source[x, y]
            high = value.astype(jnp.bfloat16)
            low = (value - high.astype(F32)).astype(jnp.bfloat16)
            both = jnp.concatenate([high, low], axis=0)
            for b in range(nb):
                out = lax.dot_general(
                    both[:, b * blk : (b + 1) * blk],
                    inv[x, y, b],
                    (((1,), (0,)), ((), ())),
                    preferred_element_type=F32,
                )
                out = out[:kk] + out[kk:]
                zs[i, x, y, :, b * blk : (b + 1) * blk] = out if i == 0 else out * BASIS_SCALE

    first_x, first_y = me_w * cx, me_n * cy
    def remote(source, target, send, recv, device):
        return pltpu.make_async_remote_copy(
            src_ref=source, dst_ref=target, send_sem=send, recv_sem=recv, device_id=device, device_id_type=MESH
        )

    def copy_x(i, side, c):
        ys = pl.ds(c * wide_y, wide_y)
        source, device = ((cx - 1, {"wide": right}), (0, {"wide": left}))[side]
        send, recv = halo_send.at[i, 2 + 2 * c + side], halo_recv.at[i, 2 + 2 * c + side]
        return remote(zs.at[i, source, ys], halo_x.at[i, side, ys], send, recv, device)

    def copy_y(i, side):
        source, device = ((cy - 1, {"narrow": above}), (0, {"narrow": below}))[side]
        return remote(zs.at[i, :, source], halo_y.at[i, side], halo_send.at[i, side], halo_recv.at[i, side], device)

    def emit(i, c):
        copy_x(i, 0, c).start()
        copy_x(i, 1, c).start()
        if c == CHUNKS - 1:
            copy_y(i, 0).start()
        if c == 0:
            copy_y(i, 1).start()

    coef_copies = [
        remote(coef.at[cx - 1], coef_x.at[0], coef_send.at[0], coef_recv.at[0], {"wide": right}),
        remote(coef.at[0], coef_x.at[1], coef_send.at[1], coef_recv.at[1], {"wide": left}),
        remote(coef, coef_y.at[0], coef_send.at[2], coef_recv.at[2], {"narrow": above}),
        remote(coef, coef_y.at[1], coef_send.at[3], coef_recv.at[3], {"narrow": below}),
    ]
    for copy in coef_copies:
        copy.start()
    for c in order:
        for load in chunk_loads[c]:
            load.wait()
        for x, y in chunk(c):
            here = (first_x + x) * (n_narrow * cy) + first_y + y
            rhs[x, y] = rhs[x, y] + jnp.where(well_of == here, WELL_RATE, 0.0)
        precondition(rhs, 0, c)
        emit(0, c)
    for axis in ("wide", "narrow"):
        hear(axis, 0)
        tell(axis, 1)

    has_left = jnp.where(me_w == 0, 0.0, 1.0)
    has_right = jnp.where(me_w == n_wide - 1, 0.0, 1.0)
    has_below = jnp.where(me_n == 0, 0.0, 1.0)
    has_above = jnp.where(me_n == n_narrow - 1, 0.0, 1.0)

    def spread(line):
        return jnp.broadcast_to(line, (8, nz))

    for x, y in columns:
        coef_pad[x + 1, y + 1] = spread(coef[x, y : y + 1])
    lane8 = lax.broadcasted_iota(jnp.int32, (8, nz), 1)

    def next_layer(value):
        return jnp.where(lane8 == nz - 1, 0.0, pltpu.roll(value, nz - 1, 1))

    def last_layer(value):
        return jnp.where(lane8 == 0, 0.0, pltpu.roll(value, 1, 1))

    def coupled(x, y):
        if x > 0:
            yield (x, y + 1), (x - 1, y)
        if x < cx - 1:
            yield (x + 2, y + 1), (x + 1, y)
        if y > 0:
            yield (x + 1, y), (x, y - 1)
        if y < cy - 1:
            yield (x + 1, y + 2), (x, y + 1)

    for x, y in columns:
        c = coef_pad[x + 1, y + 1]
        around = next_layer(c) + last_layer(c)
        for at, _ in coupled(x, y):
            around += coef_pad[at]
        dfull[x, y] = spread(diag[x, y : y + 1]) + c * around

    def operate_inside(i):
        for x, y in columns:
            c = coef_pad[x + 1, y + 1]
            for h in range(kk // 8):
                ks = pl.ds(8 * h, 8)
                v = zs[i, x, y, ks]
                u = c * v
                near = next_layer(u) + last_layer(u)
                for at, (nx, ny) in coupled(x, y):
                    near += coef_pad[at] * zs[i, nx, ny, ks]
                ws[i, x, y, ks] = dfull[x, y] * v - c * near

    def absorb(i, c):
        copy_x(i, 0, c).wait()
        copy_x(i, 1, c).wait()
        if c == 0:
            copy_y(i, 0).wait()
        if c == CHUNKS - 1:
            copy_y(i, 1).wait()
        for x, y in chunk(c):
            edges = []
            if x == 0:
                edges.append(((0, y + 1), halo_x.at[i, 0, y]))
            if x == cx - 1:
                edges.append(((cx + 1, y + 1), halo_x.at[i, 1, y]))
            if y == 0:
                edges.append(((x + 1, 0), halo_y.at[i, 0, x]))
            if y == cy - 1:
                edges.append(((x + 1, cy + 1), halo_y.at[i, 1, x]))
            both = [coef_pad[x + 1, y + 1] * coef_pad[at] for at, _ in edges]
            for h in range(kk // 8):
                ks = pl.ds(8 * h, 8)
                v, w = zs[i, x, y, ks], ws[i, x, y, ks]
                for pair, (_, outer) in zip(both, edges):
                    w += pair * (v - outer[ks])
                ws[i, x, y, ks] = w

    def gram(lefts, rights):
        acc = None
        for x, y in columns:
            left_rows = jnp.concatenate([ref[x, y] for ref in lefts], axis=0)
            right_rows = jnp.concatenate([ref[x, y] for ref in rights], axis=0)
            product = dot_nt(left_rows, right_rows, SPLIT)
            acc = product if acc is None else acc + product
        return acc

    def send_all(axis, me, count, source, target, send, recv):
        def send_to(d):
            peer = lax.rem(me + d, count)
            remote(source, target.at[d - 1], send, recv, {axis: peer}).start()

        send_to(count // 2)

        @pl.loop(1, count // 2)
        def _(t):
            send_to(count // 2 - t)
            send_to(count // 2 + t)

    def received(axis, peer, target, send, recv):
        done = remote(target, target, send, recv, {axis: peer})
        done.wait_recv()
        done.wait_send()

    def add_all(own, target):
        lines = [own] + [target[d] for d in range(target.shape[0])]
        while len(lines) > 1:
            lines = [a + b for a, b in zip(lines[::2], lines[1::2])] + lines[len(lines) // 2 * 2 :]
        return lines[0]

    sums = [(part, wide_in, plane, plane_in), (part, wide_in, plane, plane_in), (part_c, wide_in_c, plane_c, plane_in_c)]
    slot = [0, 1, 0]

    def sum_wide(j, value):
        own, into = sums[j][0].at[slot[j]], sums[j][1].at[slot[j]]
        own[...] = value
        send_all("wide", me_w, n_wide, own, into, sum_send.at[j, 0], sum_recv.at[j, 0])

    def sum_narrow(j):
        own, into, mid, last = (ref.at[slot[j]] for ref in sums[j])
        received("wide", right, into, sum_send.at[j, 0], sum_recv.at[j, 0])
        mid[...] = add_all(own[...], into)
        send_all("narrow", me_n, n_narrow, mid, last, sum_send.at[j, 1], sum_recv.at[j, 1])

    def sum_done(j):
        mid, last = sums[j][2].at[slot[j]], sums[j][3].at[slot[j]]
        received("narrow", above, last, sum_send.at[j, 1], sum_recv.at[j, 1])
        return add_all(mid[...], last)

    z_refs = [zs.at[i] for i in range(BASIS)]
    w_refs = [ws.at[i] for i in range(BASIS)]

    def halve(line):
        return jnp.concatenate([line[:8], line[8:]], axis=1)

    for i in range(BASIS):
        if i > 0:
            for c in order:
                absorb(i - 1, c)
                precondition(w_refs[i - 1], i, c)
                emit(i, c)
        if i == 1:
            hear("wide", 2)
            tell("wide", 3)
            hear("narrow", 1)
            tell("narrow", 2)
        operate_inside(i)
        if i == 0:
            for copy in coef_copies:
                copy.wait()
            for y in range(cy):
                coef_pad[0, y + 1] = spread(coef_x[0, y : y + 1] * has_left)
                coef_pad[cx + 1, y + 1] = spread(coef_x[1, y : y + 1] * has_right)
            for x in range(cx):
                coef_pad[x + 1, 0] = spread(coef_y[0, x, cy - 1 : cy] * has_below)
                coef_pad[x + 1, cy + 1] = spread(coef_y[1, x, 0:1] * has_above)
        if i == 0:
            hear("wide", 1)
            tell("wide", 2)
        if i == 1:
            first = gram([rhs, w_refs[0]], [z_refs[0], z_refs[1]])
            hear("wide", 3)
            sum_wide(0, halve(jnp.concatenate([first[:kk], first[kk:]], axis=1)))
        if i == 2:
            second = gram([rhs, w_refs[0], w_refs[1]], [z_refs[1], z_refs[2]])
            line = [second[:kk, kk:], second[kk : 2 * kk, kk:], second[2 * kk :]]
            sum_wide(1, halve(jnp.concatenate(line, axis=1)))
            hear("narrow", 2)
            sum_narrow(0)
    for c in order:
        absorb(BASIS - 1, c)

    lanes = lax.broadcasted_iota(jnp.int32, (kk, 128), 1)
    rows = lax.broadcasted_iota(jnp.int32, (kk, 128), 0)
    diagonal = lanes // kk == lax.rem(rows, 8)
    third = gram([w_refs[2]], [z_refs[2]])
    third = jnp.where(diagonal, jnp.concatenate([third] * 8, axis=1), 0.0)
    sum_wide(2, jnp.concatenate([jnp.sum(third[:8], axis=0, keepdims=True), jnp.sum(third[8:], axis=0, keepdims=True)], axis=0))

    matrix[...] = jnp.zeros_like(matrix)
    sum_narrow(1)
    first = sum_done(0)
    for h in range(2):
        matrix[8 * h : 8 * h + 8, 0 : 2 * kk] = first[:, 64 * h : 64 * h + 2 * kk]
        matrix[kk + 8 * h : kk + 8 * h + 8, 0 : 2 * kk] = first[:, 64 * h + 2 * kk : 64 * h + 4 * kk]
    sum_narrow(2)
    second = sum_done(1)
    for h in range(2):
        for r in range(2):
            piece = second[:, 64 * h + r * kk : 64 * h + (r + 1) * kk]
            matrix[r * kk + 8 * h : r * kk + 8 * h + 8, 2 * kk : 3 * kk] = piece
        matrix[2 * kk + 8 * h : 2 * kk + 8 * h + 8, kk : 3 * kk] = second[:, 64 * h + 2 * kk : 64 * h + 4 * kk]
    pick_rows = lax.broadcasted_iota(jnp.int32, (2 * kk, 128), 0)
    pick_lanes = lax.broadcasted_iota(jnp.int32, (2 * kk, 128), 1)
    pick = jnp.where(pick_lanes == pick_rows + kk, 1.0, 0.0)
    matrix[2 * kk :, 0 : 2 * kk] = dot_nt(pick, matrix[kk : 3 * kk])

    lane = lax.broadcasted_iota(jnp.int32, (1, 128), 1)

    def eliminate(system, row, k):
        shape = system.shape
        c0 = jnp.broadcast_to(system[:, k : k + 1], shape)
        c1 = jnp.broadcast_to(system[:, k + 1 : k + 2], shape)
        p0, p1 = system[row : row + 1], system[row + 1 : row + 2]
        a, b = c0[row : row + 1], c1[row : row + 1]
        c, d = c0[row + 1 : row + 2], c1[row + 1 : row + 2]
        inverse = 1.0 / (a * d - b * c)
        at0, at1 = lane == k, lane == k + 1
        g0 = jnp.where(at0, -d, jnp.where(at1, b, d * p0 - b * p1)) * inverse
        g1 = jnp.where(at0, c, jnp.where(at1, -a, a * p1 - c * p0)) * inverse
        kept = jnp.where(at0 | at1, 0.0, system)
        return kept - c0 * g0 - c1 * g1

    system = matrix[...]
    for k in range(0, 2 * kk, 2):
        system = eliminate(system, kk + k, k)

    third = sum_done(2)
    third = jnp.concatenate([jnp.broadcast_to(third[h : h + 1], (8, 128)) for h in range(2)], axis=0)
    third = jnp.where(diagonal, third, 0.0)
    for shift in (64, 32, 16):
        third = third + pltpu.roll(third, shift, 1)
    third = jnp.where((lanes >= 2 * kk) & (lanes < 3 * kk), third, 0.0)
    system = jnp.concatenate([system[:kk], system[3 * kk :] + third], axis=0)
    for k in range(0, kk, 2):
        system = eliminate(system, kk + k, 2 * kk + k)
    weights[...] = system[:kk]


def combine(weights, rhs, zs, ws, sol_hbm, res_hbm, sol, res, sol_turned, res_turned, out_sem):
    cx, cy, kk, nz = rhs.shape
    y = weights[:, : BASIS * kk]
    copies = []
    for x in range(cx):
        for yy in range(cy):
            basis = jnp.concatenate([zs[i, x, yy] for i in range(BASIS)], axis=0)
            image = jnp.concatenate([ws[i, x, yy] for i in range(BASIS)], axis=0)
            sol[x, yy] = dot_nn(y, basis)
            res[x, yy] = rhs[x, yy] - dot_nn(y, image)
        for buffer, turned, target in ((sol, sol_turned, sol_hbm), (res, res_turned, res_hbm)):
            turned[x] = jnp.swapaxes(buffer[x], 0, 1)
            copy = pltpu.make_async_copy(turned.at[x], target.at[:, x], out_sem.at[len(copies)])
            copy.start()
            copies.append(copy)
    for copy in copies:
        copy.wait()


def solution(mesh):
    n_wide, n_narrow = mesh.shape["wide"], mesh.shape["narrow"]

    def on_device(sources, well_columns, column_active, perm_root, storage_term, inverse_blocks):
        kk, cx, cy, nz = sources.shape
        nb, blk = inverse_blocks.shape[2], inverse_blocks.shape[3]
        dma = pltpu.SemaphoreType.DMA
        vmem = pltpu.VMEM
        held = pl.pallas_call(
            functools.partial(kernel, n_wide, n_narrow),
            out_shape=(
                vmem((kk, 128), F32),
                vmem((cx, cy, kk, nz), F32),
                vmem((BASIS, cx, cy, kk, nz), F32),
                vmem((BASIS, cx, cy, kk, nz), F32),
            ),
            in_specs=[pl.BlockSpec(memory_space=pl.ANY)] * 6,
            out_specs=(pl.BlockSpec(memory_space=vmem),) * 4,
            scratch_shapes=[
                pltpu.SMEM(well_columns.shape, jnp.int32),
                pltpu.SMEM(column_active.shape, jnp.int32),
                vmem((cx, cy, nz), F32),
                vmem((cx, cy, nz), F32),
                vmem(inverse_blocks.shape, inverse_blocks.dtype),
                vmem((cx, cy, nz), F32),
                vmem((2, cx, cy, nz), F32),
                vmem((2, cy, nz), F32),
                vmem((cx + 2, cy + 2, 8, nz), F32),
                vmem((cx, cy, nz), F32),
                vmem((BASIS, 2, cy, kk, nz), F32),
                vmem((BASIS, 2, cx, kk, nz), F32),
                vmem((2, 8, 128), F32),
                vmem((2, n_wide - 1, 8, 128), F32),
                vmem((2, 8, 128), F32),
                vmem((2, n_narrow - 1, 8, 128), F32),
                vmem((1, 2, 128), F32),
                vmem((1, n_wide - 1, 2, 128), F32),
                vmem((1, 2, 128), F32),
                vmem((1, n_narrow - 1, 2, 128), F32),
                vmem(((BASIS + 1) * kk, 128), F32),
                vmem((cx, cy, 8, nz), F32),
                dma((4 + CHUNKS * cx + cx * cy,)),
                dma((4,)),
                dma((4,)),
                dma((BASIS, 2 + 2 * CHUNKS)),
                dma((BASIS, 2 + 2 * CHUNKS)),
                dma((3, 2)),
                dma((3, 2)),
                pltpu.SemaphoreType.REGULAR((2, 4)),
            ],
            compiler_params=pltpu.CompilerParams(collective_id=0, has_side_effects=True),
        )(sources, well_columns, column_active, perm_root, storage_term, inverse_blocks)
        field = jax.ShapeDtypeStruct(sources.shape, F32)
        return pl.pallas_call(
            combine,
            out_shape=(field, field),
            in_specs=[pl.BlockSpec(memory_space=vmem)] * 4,
            out_specs=(pl.BlockSpec(memory_space=pl.ANY),) * 2,
            scratch_shapes=[
                vmem((cx, cy, kk, nz), F32),
                vmem((cx, cy, kk, nz), F32),
                vmem((cx, kk, cy, nz), F32),
                vmem((cx, kk, cy, nz), F32),
                dma((2 * cx,)),
            ],
        )(*(pltpu.with_memory_space_constraint(value, vmem) for value in held))

    in_specs = (
        P(None, "wide", "narrow", None),
        P(),
        P("wide", "narrow"),
        P("wide", "narrow", None),
        P("wide", "narrow", None),
        P("wide", "narrow", None, None, None),
    )
    out_specs = (P(None, "wide", "narrow", None), P(None, "wide", "narrow", None))
    return jax.shard_map(
        on_device, mesh=mesh, in_specs=in_specs, out_specs=out_specs, check_vma=False
    )
```

```python
import functools

import jax
import jax.numpy as jnp
from jax import lax
from jax.experimental import pallas as pl
from jax.experimental.pallas import tpu as pltpu
from jax.sharding import PartitionSpec as P

BASIS = 3
WELL_RATE = 4.0
BASIS_SCALE = 1.0 / 16.0
MESH = pl.DeviceIdType.MESH
EXACT = lax.Precision.HIGHEST
SPLIT = lax.Precision.HIGH
CHUNKS = 4
F32 = jnp.float32


def dot_nt(left, right, precision=EXACT):
    return lax.dot_general(left, right, (((1,), (1,)), ((), ())), precision=precision, preferred_element_type=F32)


def kernel(
    n_wide,
    n_narrow,
    src_hbm,
    wells_hbm,
    active_hbm,
    perm_hbm,
    storage_hbm,
    inv_hbm,
    weights,
    rhs,
    split,
    wells,
    active,
    perm,
    storage,
    inv,
    coef,
    coef_y,
    coef_x,
    coef_pad,
    diag,
    zs,
    ws,
    halo_x,
    halo_y,
    part,
    wide_in,
    plane,
    plane_in,
    part_b,
    wide_in_b,
    plane_b,
    plane_in_b,
    part_c,
    wide_in_c,
    plane_c,
    plane_in_c,
    matrix,
    dfull,
    load_sem,
    coef_send,
    coef_recv,
    halo_send,
    halo_recv,
    sum_send,
    sum_recv,
    tokens,
):
    kk, cx, cy, nz = src_hbm.shape
    blk = inv_hbm.shape[-1]
    nb = inv_hbm.shape[2]
    me_w, me_n = lax.axis_index("wide"), lax.axis_index("narrow")
    right, left = lax.rem(me_w + 1, n_wide), lax.rem(me_w + n_wide - 1, n_wide)
    above, below = lax.rem(me_n + 1, n_narrow), lax.rem(me_n + n_narrow - 1, n_narrow)

    barrier = pltpu.get_barrier_semaphore()

    for axis, peer in (("wide", right), ("wide", left), ("narrow", above), ("narrow", below)):
        pl.semaphore_signal(barrier, inc=1, device_id={axis: peer}, device_id_type=MESH)

    rings = {"wide": (0, me_w, n_wide), "narrow": (1, me_n, n_narrow)}

    def tell(axis, r):
        at, me, count = rings[axis]
        for d in (2**r, count - 2**r):
            peer = lax.rem(me + d, count)
            pl.semaphore_signal(tokens.at[at, r], inc=1, device_id={axis: peer}, device_id_type=MESH)

    def hear(axis, r):
        pl.semaphore_wait(tokens.at[rings[axis][0], r], 2)

    loads = [
        pltpu.make_async_copy(wells_hbm, wells, load_sem.at[0]),
        pltpu.make_async_copy(active_hbm, active, load_sem.at[1]),
        pltpu.make_async_copy(perm_hbm, perm, load_sem.at[2]),
        pltpu.make_async_copy(storage_hbm, storage, load_sem.at[3]),
    ]
    wide_y = cy // CHUNKS
    order = [0, CHUNKS - 1] + list(range(1, CHUNKS - 1))

    def chunk(c):
        return [(x, y) for x in reversed(range(cx)) for y in range(c * wide_y, (c + 1) * wide_y)]

    columns = [(x, y) for x in range(cx) for y in range(cy)]
    chunk_loads = {}
    for c in order:
        ys = pl.ds(c * wide_y, wide_y)
        own = [(inv_hbm.at[x, ys], inv.at[x, ys]) for x in range(cx)]
        own += [(src_hbm.at[:, x, y, :], rhs.at[x, y]) for x, y in chunk(c)]
        first = 4 + c * len(own)
        chunk_loads[c] = [
            pltpu.make_async_copy(source, target, load_sem.at[first + at]) for at, (source, target) in enumerate(own)
        ]
    for load in loads + [load for c in order for load in chunk_loads[c]]:
        load.start()
    pl.semaphore_wait(barrier, 4)
    tell("wide", 0)
    tell("narrow", 0)
    for load in loads:
        load.wait()

    row = lax.broadcasted_iota(jnp.int32, (cy, nz), 0)
    for x in range(cx):
        on = jnp.zeros((cy, nz), F32)
        for y in range(cy):
            on = jnp.where(row == y, active[x, y].astype(F32), on)
        coef[x] = perm[x] * on
        diag[x] = on * storage[x] + (1.0 - on)

    ids = lax.broadcasted_iota(jnp.int32, (kk, nz), 0)
    well_of = jnp.zeros((kk, nz), jnp.int32)
    for k in range(kk):
        well_of = jnp.where(ids == k, wells[k], well_of)

    def precondition(source, i, c):
        for x, y in chunk(c):
            value = source[x, y]
            high = value.astype(jnp.bfloat16)
            low = (value - high.astype(F32)).astype(jnp.bfloat16)
            both = jnp.concatenate([high, low], axis=0)
            for b in range(nb):
                out = lax.dot_general(
                    both[:, b * blk : (b + 1) * blk],
                    inv[x, y, b],
                    (((1,), (0,)), ((), ())),
                    preferred_element_type=F32,
                )
                out = out[:kk] + out[kk:]
                zs[i, x, y, :, b * blk : (b + 1) * blk] = out if i == 0 else out * BASIS_SCALE

    first_x, first_y = me_w * cx, me_n * cy
    def remote(source, target, send, recv, device):
        return pltpu.make_async_remote_copy(
            src_ref=source, dst_ref=target, send_sem=send, recv_sem=recv, device_id=device, device_id_type=MESH
        )

    def copy_x(i, side, c):
        ys = pl.ds(c * wide_y, wide_y)
        source, device = ((cx - 1, {"wide": right}), (0, {"wide": left}))[side]
        send, recv = halo_send.at[i, 2 + 2 * c + side], halo_recv.at[i, 2 + 2 * c + side]
        return remote(zs.at[i, source, ys], halo_x.at[i, side, ys], send, recv, device)

    def copy_y(i, side):
        source, device = ((cy - 1, {"narrow": above}), (0, {"narrow": below}))[side]
        return remote(zs.at[i, :, source], halo_y.at[i, side], halo_send.at[i, side], halo_recv.at[i, side], device)

    def emit(i, c):
        copy_x(i, 0, c).start()
        copy_x(i, 1, c).start()
        if c == CHUNKS - 1:
            copy_y(i, 0).start()
        if c == 0:
            copy_y(i, 1).start()

    coef_copies = [
        remote(coef.at[cx - 1], coef_x.at[0], coef_send.at[0], coef_recv.at[0], {"wide": right}),
        remote(coef.at[0], coef_x.at[1], coef_send.at[1], coef_recv.at[1], {"wide": left}),
        remote(coef, coef_y.at[0], coef_send.at[2], coef_recv.at[2], {"narrow": above}),
        remote(coef, coef_y.at[1], coef_send.at[3], coef_recv.at[3], {"narrow": below}),
    ]
    for copy in coef_copies:
        copy.start()
    for c in order:
        for load in chunk_loads[c]:
            load.wait()
        for x, y in chunk(c):
            here = (first_x + x) * (n_narrow * cy) + first_y + y
            rhs[x, y] = rhs[x, y] + jnp.where(well_of == here, WELL_RATE, 0.0)
        precondition(rhs, 0, c)
        emit(0, c)
    for axis in ("wide", "narrow"):
        hear(axis, 0)
        tell(axis, 1)

    has_left = jnp.where(me_w == 0, 0.0, 1.0)
    has_right = jnp.where(me_w == n_wide - 1, 0.0, 1.0)
    has_below = jnp.where(me_n == 0, 0.0, 1.0)
    has_above = jnp.where(me_n == n_narrow - 1, 0.0, 1.0)

    def spread(line):
        return jnp.broadcast_to(line, (8, nz))

    for x, y in columns:
        coef_pad[x + 1, y + 1] = spread(coef[x, y : y + 1])
    lane8 = lax.broadcasted_iota(jnp.int32, (8, nz), 1)

    def next_layer(value):
        return jnp.where(lane8 == nz - 1, 0.0, pltpu.roll(value, nz - 1, 1))

    def last_layer(value):
        return jnp.where(lane8 == 0, 0.0, pltpu.roll(value, 1, 1))

    def coupled(x, y):
        if x > 0:
            yield (x, y + 1), (x - 1, y)
        if x < cx - 1:
            yield (x + 2, y + 1), (x + 1, y)
        if y > 0:
            yield (x + 1, y), (x, y - 1)
        if y < cy - 1:
            yield (x + 1, y + 2), (x, y + 1)

    for x, y in columns:
        c = coef_pad[x + 1, y + 1]
        around = next_layer(c) + last_layer(c)
        for at, _ in coupled(x, y):
            around += coef_pad[at]
        dfull[x, y] = spread(diag[x, y : y + 1]) + c * around

    def operate_inside(i):
        for x, y in columns:
            c = coef_pad[x + 1, y + 1]
            for h in range(kk // 8):
                ks = pl.ds(8 * h, 8)
                v = zs[i, x, y, ks]
                u = c * v
                near = next_layer(u) + last_layer(u)
                for at, (nx, ny) in coupled(x, y):
                    near += coef_pad[at] * zs[i, nx, ny, ks]
                ws[i, x, y, ks] = dfull[x, y] * v - c * near

    def absorb(i, c):
        copy_x(i, 0, c).wait()
        copy_x(i, 1, c).wait()
        if c == 0:
            copy_y(i, 0).wait()
        if c == CHUNKS - 1:
            copy_y(i, 1).wait()
        for x, y in chunk(c):
            edges = []
            if x == 0:
                edges.append(((0, y + 1), halo_x.at[i, 0, y]))
            if x == cx - 1:
                edges.append(((cx + 1, y + 1), halo_x.at[i, 1, y]))
            if y == 0:
                edges.append(((x + 1, 0), halo_y.at[i, 0, x]))
            if y == cy - 1:
                edges.append(((x + 1, cy + 1), halo_y.at[i, 1, x]))
            both = [coef_pad[x + 1, y + 1] * coef_pad[at] for at, _ in edges]
            for h in range(kk // 8):
                ks = pl.ds(8 * h, 8)
                v, w = zs[i, x, y, ks], ws[i, x, y, ks]
                for pair, (_, outer) in zip(both, edges):
                    w += pair * (v - outer[ks])
                ws[i, x, y, ks] = w

    def gram(lefts, rights, cells, acc=None):
        for x, y in cells:
            left_rows = jnp.concatenate([ref[x, y] for ref in lefts], axis=0)
            right_rows = jnp.concatenate([ref[x, y] for ref in rights], axis=0)
            product = dot_nt(left_rows, right_rows, SPLIT)
            acc = product if acc is None else acc + product
        return acc

    def send_all(axis, me, count, source, target, send, recv):
        def send_to(d):
            peer = lax.rem(me + d, count)
            remote(source, target.at[d - 1], send, recv, {axis: peer}).start()

        send_to(count // 2)

        @pl.loop(1, count // 2)
        def _(t):
            send_to(count // 2 - t)
            send_to(count // 2 + t)

    def received(axis, peer, target, send, recv):
        done = remote(target, target, send, recv, {axis: peer})
        done.wait_recv()
        done.wait_send()

    def add_all(own, target):
        lines = [own] + [target[d] for d in range(target.shape[0])]
        while len(lines) > 1:
            lines = [a + b for a, b in zip(lines[::2], lines[1::2])] + lines[len(lines) // 2 * 2 :]
        return lines[0]

    sums = [
        (part, wide_in, plane, plane_in),
        (part_b, wide_in_b, plane_b, plane_in_b),
        (part_c, wide_in_c, plane_c, plane_in_c),
    ]

    def sum_wide(j, value):
        own, into = sums[j][0], sums[j][1]
        own[...] = value
        send_all("wide", me_w, n_wide, own, into, sum_send.at[j, 0], sum_recv.at[j, 0])

    def sum_narrow(j):
        own, into, mid, last = sums[j]
        received("wide", right, into, sum_send.at[j, 0], sum_recv.at[j, 0])
        mid[...] = add_all(own[...], into)
        send_all("narrow", me_n, n_narrow, mid, last, sum_send.at[j, 1], sum_recv.at[j, 1])

    def sum_done(j):
        mid, last = sums[j][2], sums[j][3]
        received("narrow", above, last, sum_send.at[j, 1], sum_recv.at[j, 1])
        return add_all(mid[...], last)

    z_refs = [zs.at[i] for i in range(BASIS)]
    w_refs = [ws.at[i] for i in range(BASIS)]

    def halve(line):
        return jnp.concatenate([line[:8], line[8:]], axis=1)

    for i in range(BASIS):
        if i > 0:
            for c in order:
                absorb(i - 1, c)
                precondition(w_refs[i - 1], i, c)
                emit(i, c)
        if i == 1:
            hear("wide", 2)
            tell("wide", 3)
            hear("narrow", 1)
            tell("narrow", 2)
        operate_inside(i)
        if i == 0:
            for copy in coef_copies:
                copy.wait()
            for y in range(cy):
                coef_pad[0, y + 1] = spread(coef_x[0, y : y + 1] * has_left)
                coef_pad[cx + 1, y + 1] = spread(coef_x[1, y : y + 1] * has_right)
            for x in range(cx):
                coef_pad[x + 1, 0] = spread(coef_y[0, x, cy - 1 : cy] * has_below)
                coef_pad[x + 1, cy + 1] = spread(coef_y[1, x, 0:1] * has_above)
        if i == 0:
            hear("wide", 1)
            tell("wide", 2)
        if i == 1:
            first = gram([rhs, w_refs[0]], [z_refs[0], z_refs[1]], columns)
            hear("wide", 3)
            sum_wide(0, halve(jnp.concatenate([first[:kk], first[kk:]], axis=1)))
        if i == 2:
            second = gram([w_refs[1]], [z_refs[1], z_refs[2]], columns)
            sum_wide(1, jnp.concatenate([second[at : at + 4] for at in range(0, kk, 4)], axis=1))
            hear("narrow", 2)
            sum_narrow(0)
    third = None
    for c in order:
        absorb(BASIS - 1, c)
        third = gram([w_refs[2]], [z_refs[2]], chunk(c), third)

    lanes = lax.broadcasted_iota(jnp.int32, (kk, 128), 1)
    rows = lax.broadcasted_iota(jnp.int32, (kk, 128), 0)
    diagonal = lanes // kk == lax.rem(rows, 8)
    third = jnp.where(diagonal, jnp.concatenate([third] * 8, axis=1), 0.0)
    sum_wide(2, jnp.concatenate([jnp.sum(third[:8], axis=0, keepdims=True), jnp.sum(third[8:], axis=0, keepdims=True)], axis=0))

    for x, yy in columns:
        for at, field in enumerate((zs, ws)):
            value = jnp.concatenate([field[i, x, yy] for i in range(BASIS)], axis=0)
            high = value.astype(jnp.bfloat16)
            split[at, x, yy, : BASIS * kk] = high
            split[at, x, yy, BASIS * kk :] = (value - high.astype(F32)).astype(jnp.bfloat16)

    matrix[...] = jnp.zeros_like(matrix)
    sum_narrow(1)
    first = sum_done(0)
    for h in range(2):
        matrix[8 * h : 8 * h + 8, 0 : 2 * kk] = first[:, 64 * h : 64 * h + 2 * kk]
        matrix[kk + 8 * h : kk + 8 * h + 8, 0 : 2 * kk] = first[:, 64 * h + 2 * kk : 64 * h + 4 * kk]
    sum_narrow(2)
    for h in range(2):
        piece = first[:, 64 * h + 3 * kk : 64 * h + 4 * kk]
        matrix[8 * h : 8 * h + 8, 2 * kk : 3 * kk] = piece * BASIS_SCALE
    second = sum_done(1)
    for g in range(4):
        piece = second[:, 2 * kk * g : 2 * kk * (g + 1)]
        matrix[2 * kk + 4 * g : 2 * kk + 4 * g + 4, kk : 3 * kk] = piece
        matrix[kk + 4 * g : kk + 4 * g + 4, 2 * kk : 3 * kk] = piece[:, :kk]
    pick_rows = lax.broadcasted_iota(jnp.int32, (2 * kk, 128), 0)
    pick_lanes = lax.broadcasted_iota(jnp.int32, (2 * kk, 128), 1)
    pick = jnp.where(pick_lanes == pick_rows + kk, 1.0, 0.0)
    matrix[2 * kk :, 0 : 2 * kk] = dot_nt(pick, matrix[kk : 3 * kk])

    lane = lax.broadcasted_iota(jnp.int32, (1, 128), 1)

    def eliminate(system, row, k):
        shape = system.shape
        c0 = jnp.broadcast_to(system[:, k : k + 1], shape)
        c1 = jnp.broadcast_to(system[:, k + 1 : k + 2], shape)
        p0, p1 = system[row : row + 1], system[row + 1 : row + 2]
        a, b = c0[row : row + 1], c1[row : row + 1]
        c, d = c0[row + 1 : row + 2], c1[row + 1 : row + 2]
        inverse = 1.0 / (a * d - b * c)
        at0, at1 = lane == k, lane == k + 1
        g0 = jnp.where(at0, -d, jnp.where(at1, b, d * p0 - b * p1)) * inverse
        g1 = jnp.where(at0, c, jnp.where(at1, -a, a * p1 - c * p0)) * inverse
        kept = jnp.where(at0 | at1, 0.0, system)
        return kept - c0 * g0 - c1 * g1

    system = matrix[...]
    for k in range(0, 2 * kk, 2):
        system = eliminate(system, kk + k, k)

    third = sum_done(2)
    third = jnp.concatenate([jnp.broadcast_to(third[h : h + 1], (8, 128)) for h in range(2)], axis=0)
    third = jnp.where(diagonal, third, 0.0)
    for shift in (64, 32, 16):
        third = third + pltpu.roll(third, shift, 1)
    third = jnp.where((lanes >= 2 * kk) & (lanes < 3 * kk), third, 0.0)
    system = jnp.concatenate([system[:kk], system[3 * kk :] + third], axis=0)
    for k in range(0, kk, 2):
        system = eliminate(system, kk + k, 2 * kk + k)
    weights[...] = system[:kk]


def combine(weights, rhs, split, sol_hbm, res_hbm, sol, res, sol_turned, res_turned, out_sem):
    cx, cy, kk, nz = rhs.shape
    y = weights[:, : BASIS * kk]
    high = y.astype(jnp.bfloat16)
    low = (y - high.astype(F32)).astype(jnp.bfloat16)
    factors = jnp.concatenate(
        [jnp.concatenate([high, high], axis=1), jnp.concatenate([low, jnp.zeros_like(low)], axis=1)], axis=0
    )

    def weighted(at, x, yy):
        out = lax.dot_general(
            factors, split[at, x, yy], (((1,), (0,)), ((), ())), preferred_element_type=F32
        )
        return out[:kk] + out[kk:]

    copies = []
    for x in range(cx):
        for yy in range(cy):
            sol[x, yy] = weighted(0, x, yy)
            res[x, yy] = rhs[x, yy] - weighted(1, x, yy)
        for buffer, turned, target in ((sol, sol_turned, sol_hbm), (res, res_turned, res_hbm)):
            turned[x] = jnp.swapaxes(buffer[x], 0, 1)
            copy = pltpu.make_async_copy(turned.at[x], target.at[:, x], out_sem.at[len(copies)])
            copy.start()
            copies.append(copy)
    for copy in copies:
        copy.wait()


def solution(mesh):
    n_wide, n_narrow = mesh.shape["wide"], mesh.shape["narrow"]

    def on_device(sources, well_columns, column_active, perm_root, storage_term, inverse_blocks):
        kk, cx, cy, nz = sources.shape
        nb, blk = inverse_blocks.shape[2], inverse_blocks.shape[3]
        dma = pltpu.SemaphoreType.DMA
        vmem = pltpu.VMEM
        held = pl.pallas_call(
            functools.partial(kernel, n_wide, n_narrow),
            out_shape=(
                vmem((kk, 128), F32),
                vmem((cx, cy, kk, nz), F32),
                vmem((2, cx, cy, 2 * BASIS * kk, nz), jnp.bfloat16),
            ),
            in_specs=[pl.BlockSpec(memory_space=pl.ANY)] * 6,
            out_specs=(pl.BlockSpec(memory_space=vmem),) * 3,
            scratch_shapes=[
                pltpu.SMEM(well_columns.shape, jnp.int32),
                pltpu.SMEM(column_active.shape, jnp.int32),
                vmem((cx, cy, nz), F32),
                vmem((cx, cy, nz), F32),
                vmem(inverse_blocks.shape, inverse_blocks.dtype),
                vmem((cx, cy, nz), F32),
                vmem((2, cx, cy, nz), F32),
                vmem((2, cy, nz), F32),
                vmem((cx + 2, cy + 2, 8, nz), F32),
                vmem((cx, cy, nz), F32),
                vmem((BASIS, cx, cy, kk, nz), F32),
                vmem((BASIS, cx, cy, kk, nz), F32),
                vmem((BASIS, 2, cy, kk, nz), F32),
                vmem((BASIS, 2, cx, kk, nz), F32),
                *(
                    vmem(shape, F32)
                    for height in (8, 4, 2)
                    for shape in (
                        (height, 128),
                        (n_wide - 1, height, 128),
                        (height, 128),
                        (n_narrow - 1, height, 128),
                    )
                ),
                vmem(((BASIS + 1) * kk, 128), F32),
                vmem((cx, cy, 8, nz), F32),
                dma((4 + CHUNKS * cx + cx * cy,)),
                dma((4,)),
                dma((4,)),
                dma((BASIS, 2 + 2 * CHUNKS)),
                dma((BASIS, 2 + 2 * CHUNKS)),
                dma((3, 2)),
                dma((3, 2)),
                pltpu.SemaphoreType.REGULAR((2, 4)),
            ],
            compiler_params=pltpu.CompilerParams(collective_id=0, has_side_effects=True),
        )(sources, well_columns, column_active, perm_root, storage_term, inverse_blocks)
        field = jax.ShapeDtypeStruct(sources.shape, F32)
        return pl.pallas_call(
            combine,
            out_shape=(field, field),
            in_specs=[pl.BlockSpec(memory_space=vmem)] * 3,
            out_specs=(pl.BlockSpec(memory_space=pl.ANY),) * 2,
            scratch_shapes=[
                vmem((cx, cy, kk, nz), F32),
                vmem((cx, cy, kk, nz), F32),
                vmem((cx, kk, cy, nz), F32),
                vmem((cx, kk, cy, nz), F32),
                dma((2 * cx,)),
            ],
        )(*(pltpu.with_memory_space_constraint(value, vmem) for value in held))

    in_specs = (
        P(None, "wide", "narrow", None),
        P(),
        P("wide", "narrow"),
        P("wide", "narrow", None),
        P("wide", "narrow", None),
        P("wide", "narrow", None, None, None),
    )
    out_specs = (P(None, "wide", "narrow", None), P(None, "wide", "narrow", None))
    return jax.shard_map(
        on_device, mesh=mesh, in_specs=in_specs, out_specs=out_specs, check_vma=False
    )
```

```python
import functools

import jax
import jax.numpy as jnp
from jax import lax
from jax.experimental import pallas as pl
from jax.experimental.pallas import tpu as pltpu
from jax.sharding import PartitionSpec as P

BASIS = 3
WELL_RATE = 4.0
BASIS_SCALE = 1.0 / 16.0
MESH = pl.DeviceIdType.MESH
EXACT = lax.Precision.HIGHEST
SPLIT = lax.Precision.HIGH
CHUNKS = 4
F32 = jnp.float32


def dot_nt(left, right, precision=EXACT):
    return lax.dot_general(left, right, (((1,), (1,)), ((), ())), precision=precision, preferred_element_type=F32)


def kernel(
    n_wide,
    n_narrow,
    src_hbm,
    wells_hbm,
    active_hbm,
    perm_hbm,
    storage_hbm,
    inv_hbm,
    weights,
    rhs,
    split,
    wells,
    active,
    perm,
    storage,
    inv,
    coef,
    coef_y,
    coef_x,
    coef_pad,
    diag,
    zs,
    ws,
    halo_x,
    halo_y,
    part,
    wide_in,
    plane,
    plane_in,
    part_b,
    wide_in_b,
    plane_b,
    plane_in_b,
    part_c,
    wide_in_c,
    plane_c,
    plane_in_c,
    matrix,
    dfull,
    load_sem,
    coef_send,
    coef_recv,
    halo_send,
    halo_recv,
    sum_send,
    sum_recv,
    tokens,
):
    kk, cx, cy, nz = src_hbm.shape
    blk = inv_hbm.shape[-1]
    nb = inv_hbm.shape[2]
    me_w, me_n = lax.axis_index("wide"), lax.axis_index("narrow")
    right, left = lax.rem(me_w + 1, n_wide), lax.rem(me_w + n_wide - 1, n_wide)
    above, below = lax.rem(me_n + 1, n_narrow), lax.rem(me_n + n_narrow - 1, n_narrow)

    barrier = pltpu.get_barrier_semaphore()

    for axis, peer in (("wide", right), ("wide", left), ("narrow", above), ("narrow", below)):
        pl.semaphore_signal(barrier, inc=1, device_id={axis: peer}, device_id_type=MESH)

    rings = {"wide": (0, me_w, n_wide), "narrow": (1, me_n, n_narrow)}

    def tell(axis, r):
        at, me, count = rings[axis]
        for d in (2**r, count - 2**r):
            peer = lax.rem(me + d, count)
            pl.semaphore_signal(tokens.at[at, r], inc=1, device_id={axis: peer}, device_id_type=MESH)

    def hear(axis, r):
        pl.semaphore_wait(tokens.at[rings[axis][0], r], 2)

    loads = [
        pltpu.make_async_copy(wells_hbm, wells, load_sem.at[0]),
        pltpu.make_async_copy(active_hbm, active, load_sem.at[1]),
        pltpu.make_async_copy(perm_hbm, perm, load_sem.at[2]),
        pltpu.make_async_copy(storage_hbm, storage, load_sem.at[3]),
    ]
    wide_y = cy // CHUNKS
    order = [0, CHUNKS - 1] + list(range(1, CHUNKS - 1))

    def chunk(c):
        return [(x, y) for x in reversed(range(cx)) for y in range(c * wide_y, (c + 1) * wide_y)]

    columns = [(x, y) for x in range(cx) for y in range(cy)]
    chunk_loads = {}
    for c in order:
        ys = pl.ds(c * wide_y, wide_y)
        own = [(inv_hbm.at[x, ys], inv.at[x, ys]) for x in range(cx)]
        own += [(src_hbm.at[:, x, y, :], rhs.at[x, y]) for x, y in chunk(c)]
        first = 4 + c * len(own)
        chunk_loads[c] = [
            pltpu.make_async_copy(source, target, load_sem.at[first + at]) for at, (source, target) in enumerate(own)
        ]
    for load in loads + [load for c in order for load in chunk_loads[c]]:
        load.start()
    pl.semaphore_wait(barrier, 4)
    tell("wide", 0)
    tell("narrow", 0)
    for load in loads:
        load.wait()

    row = lax.broadcasted_iota(jnp.int32, (cy, nz), 0)
    for x in range(cx):
        on = jnp.zeros((cy, nz), F32)
        for y in range(cy):
            on = jnp.where(row == y, active[x, y].astype(F32), on)
        coef[x] = perm[x] * on
        diag[x] = on * storage[x] + (1.0 - on)

    ids = lax.broadcasted_iota(jnp.int32, (kk, nz), 0)
    well_of = jnp.zeros((kk, nz), jnp.int32)
    for k in range(kk):
        well_of = jnp.where(ids == k, wells[k], well_of)

    def precondition(source, i, c):
        for x, y in chunk(c):
            value = source[x, y]
            high = value.astype(jnp.bfloat16)
            low = (value - high.astype(F32)).astype(jnp.bfloat16)
            both = jnp.concatenate([high, low], axis=0)
            for b in range(nb):
                out = lax.dot_general(
                    both[:, b * blk : (b + 1) * blk],
                    inv[x, y, b],
                    (((1,), (0,)), ((), ())),
                    preferred_element_type=F32,
                )
                out = out[:kk] + out[kk:]
                zs[i, x, y, :, b * blk : (b + 1) * blk] = out if i == 0 else out * BASIS_SCALE

    first_x, first_y = me_w * cx, me_n * cy
    def remote(source, target, send, recv, device):
        return pltpu.make_async_remote_copy(
            src_ref=source, dst_ref=target, send_sem=send, recv_sem=recv, device_id=device, device_id_type=MESH
        )

    def copy_x(i, side, c):
        ys = pl.ds(c * wide_y, wide_y)
        source, device = ((cx - 1, {"wide": right}), (0, {"wide": left}))[side]
        send, recv = halo_send.at[i, 2 + 2 * c + side], halo_recv.at[i, 2 + 2 * c + side]
        return remote(zs.at[i, source, ys], halo_x.at[i, side, ys], send, recv, device)

    def copy_y(i, side):
        source, device = ((cy - 1, {"narrow": above}), (0, {"narrow": below}))[side]
        return remote(zs.at[i, :, source], halo_y.at[i, side], halo_send.at[i, side], halo_recv.at[i, side], device)

    def emit(i, c):
        copy_x(i, 0, c).start()
        copy_x(i, 1, c).start()
        if c == CHUNKS - 1:
            copy_y(i, 0).start()
        if c == 0:
            copy_y(i, 1).start()

    coef_copies = [
        remote(coef.at[cx - 1], coef_x.at[0], coef_send.at[0], coef_recv.at[0], {"wide": right}),
        remote(coef.at[0], coef_x.at[1], coef_send.at[1], coef_recv.at[1], {"wide": left}),
        remote(coef, coef_y.at[0], coef_send.at[2], coef_recv.at[2], {"narrow": above}),
        remote(coef, coef_y.at[1], coef_send.at[3], coef_recv.at[3], {"narrow": below}),
    ]
    for copy in coef_copies:
        copy.start()
    for c in order:
        for load in chunk_loads[c]:
            load.wait()
        for x, y in chunk(c):
            here = (first_x + x) * (n_narrow * cy) + first_y + y
            rhs[x, y] = rhs[x, y] + jnp.where(well_of == here, WELL_RATE, 0.0)
        precondition(rhs, 0, c)
        emit(0, c)
    for axis in ("wide", "narrow"):
        hear(axis, 0)
        tell(axis, 1)

    has_left = jnp.where(me_w == 0, 0.0, 1.0)
    has_right = jnp.where(me_w == n_wide - 1, 0.0, 1.0)
    has_below = jnp.where(me_n == 0, 0.0, 1.0)
    has_above = jnp.where(me_n == n_narrow - 1, 0.0, 1.0)

    def spread(line):
        return jnp.broadcast_to(line, (8, nz))

    for x, y in columns:
        coef_pad[x + 1, y + 1] = spread(coef[x, y : y + 1])
    lane8 = lax.broadcasted_iota(jnp.int32, (8, nz), 1)

    def next_layer(value):
        return jnp.where(lane8 == nz - 1, 0.0, pltpu.roll(value, nz - 1, 1))

    def last_layer(value):
        return jnp.where(lane8 == 0, 0.0, pltpu.roll(value, 1, 1))

    def coupled(x, y):
        if x > 0:
            yield (x, y + 1), (x - 1, y)
        if x < cx - 1:
            yield (x + 2, y + 1), (x + 1, y)
        if y > 0:
            yield (x + 1, y), (x, y - 1)
        if y < cy - 1:
            yield (x + 1, y + 2), (x, y + 1)

    for x, y in columns:
        c = coef_pad[x + 1, y + 1]
        around = next_layer(c) + last_layer(c)
        for at, _ in coupled(x, y):
            around += coef_pad[at]
        dfull[x, y] = spread(diag[x, y : y + 1]) + c * around

    def operate_inside(i):
        for x, y in columns:
            c = coef_pad[x + 1, y + 1]
            for h in range(kk // 8):
                ks = pl.ds(8 * h, 8)
                v = zs[i, x, y, ks]
                u = c * v
                near = next_layer(u) + last_layer(u)
                for at, (nx, ny) in coupled(x, y):
                    near += coef_pad[at] * zs[i, nx, ny, ks]
                ws[i, x, y, ks] = dfull[x, y] * v - c * near

    def absorb(i, c):
        copy_x(i, 0, c).wait()
        copy_x(i, 1, c).wait()
        if c == 0:
            copy_y(i, 0).wait()
        if c == CHUNKS - 1:
            copy_y(i, 1).wait()
        for x, y in chunk(c):
            edges = []
            if x == 0:
                edges.append(((0, y + 1), halo_x.at[i, 0, y]))
            if x == cx - 1:
                edges.append(((cx + 1, y + 1), halo_x.at[i, 1, y]))
            if y == 0:
                edges.append(((x + 1, 0), halo_y.at[i, 0, x]))
            if y == cy - 1:
                edges.append(((x + 1, cy + 1), halo_y.at[i, 1, x]))
            both = [coef_pad[x + 1, y + 1] * coef_pad[at] for at, _ in edges]
            for h in range(kk // 8):
                ks = pl.ds(8 * h, 8)
                v, w = zs[i, x, y, ks], ws[i, x, y, ks]
                for pair, (_, outer) in zip(both, edges):
                    w += pair * (v - outer[ks])
                ws[i, x, y, ks] = w

    def gram(lefts, rights, cells, acc=None):
        for x, y in cells:
            left_rows = jnp.concatenate([ref[x, y] for ref in lefts], axis=0)
            right_rows = jnp.concatenate([ref[x, y] for ref in rights], axis=0)
            product = dot_nt(left_rows, right_rows, SPLIT)
            acc = product if acc is None else acc + product
        return acc

    def send_all(axis, me, count, source, target, send, recv):
        def send_to(d):
            peer = lax.rem(me + d, count)
            remote(source, target.at[d - 1], send, recv, {axis: peer}).start()

        send_to(count // 2)

        @pl.loop(1, count // 2)
        def _(t):
            send_to(count // 2 - t)
            send_to(count // 2 + t)

    def received(axis, peer, target, send, recv):
        done = remote(target, target, send, recv, {axis: peer})
        done.wait_recv()
        done.wait_send()

    def add_all(own, target):
        lines = [own] + [target[d] for d in range(target.shape[0])]
        while len(lines) > 1:
            lines = [a + b for a, b in zip(lines[::2], lines[1::2])] + lines[len(lines) // 2 * 2 :]
        return lines[0]

    sums = [
        (part, wide_in, plane, plane_in),
        (part_b, wide_in_b, plane_b, plane_in_b),
        (part_c, wide_in_c, plane_c, plane_in_c),
    ]

    def sum_wide(j, value):
        own, into = sums[j][0], sums[j][1]
        own[...] = value
        send_all("wide", me_w, n_wide, own, into, sum_send.at[j, 0], sum_recv.at[j, 0])

    def sum_narrow(j):
        own, into, mid, last = sums[j]
        received("wide", right, into, sum_send.at[j, 0], sum_recv.at[j, 0])
        mid[...] = add_all(own[...], into)
        send_all("narrow", me_n, n_narrow, mid, last, sum_send.at[j, 1], sum_recv.at[j, 1])

    def sum_done(j):
        mid, last = sums[j][2], sums[j][3]
        received("narrow", above, last, sum_send.at[j, 1], sum_recv.at[j, 1])
        return add_all(mid[...], last)

    z_refs = [zs.at[i] for i in range(BASIS)]
    w_refs = [ws.at[i] for i in range(BASIS)]

    def halve(line):
        return jnp.concatenate([line[:8], line[8:]], axis=1)

    for i in range(BASIS):
        if i > 0:
            for c in order:
                absorb(i - 1, c)
                precondition(w_refs[i - 1], i, c)
                emit(i, c)
        if i == 1:
            hear("wide", 2)
            tell("wide", 3)
            hear("narrow", 1)
            tell("narrow", 2)
        if i == 2:
            second = gram([w_refs[1]], [z_refs[1], z_refs[2]], columns)
            sum_wide(1, jnp.concatenate([second[at : at + 4] for at in range(0, kk, 4)], axis=1))
        operate_inside(i)
        if i == 0:
            for copy in coef_copies:
                copy.wait()
            for y in range(cy):
                coef_pad[0, y + 1] = spread(coef_x[0, y : y + 1] * has_left)
                coef_pad[cx + 1, y + 1] = spread(coef_x[1, y : y + 1] * has_right)
            for x in range(cx):
                coef_pad[x + 1, 0] = spread(coef_y[0, x, cy - 1 : cy] * has_below)
                coef_pad[x + 1, cy + 1] = spread(coef_y[1, x, 0:1] * has_above)
        if i == 0:
            hear("wide", 1)
            tell("wide", 2)
        if i == 1:
            first = gram([rhs, w_refs[0]], [z_refs[0], z_refs[1]], columns)
            hear("wide", 3)
            sum_wide(0, halve(jnp.concatenate([first[:kk], first[kk:]], axis=1)))
        if i == 2:
            hear("narrow", 2)
            sum_narrow(0)
    third = None
    for c in order:
        absorb(BASIS - 1, c)
        third = gram([w_refs[2]], [z_refs[2]], chunk(c), third)

    lanes = lax.broadcasted_iota(jnp.int32, (kk, 128), 1)
    rows = lax.broadcasted_iota(jnp.int32, (kk, 128), 0)
    diagonal = lanes // kk == lax.rem(10 - lax.rem(rows, 8), 8)
    third = jnp.where(diagonal, jnp.concatenate([third] * 8, axis=1), 0.0)
    sum_wide(2, jnp.concatenate([jnp.sum(third[:8], axis=0, keepdims=True), jnp.sum(third[8:], axis=0, keepdims=True)], axis=0))

    for x, yy in columns:
        for at, field in enumerate((zs, ws)):
            value = jnp.concatenate([field[i, x, yy] for i in range(BASIS)], axis=0)
            high = value.astype(jnp.bfloat16)
            split[at, x, yy, : BASIS * kk] = high
            split[at, x, yy, BASIS * kk :] = (value - high.astype(F32)).astype(jnp.bfloat16)

    matrix[...] = jnp.zeros_like(matrix)
    sum_narrow(1)
    first = sum_done(0)
    for h in range(2):
        matrix[8 * h : 8 * h + 8, 0 : 2 * kk] = first[:, 64 * h : 64 * h + 2 * kk]
        matrix[kk + 8 * h : kk + 8 * h + 8, 0 : 2 * kk] = first[:, 64 * h + 2 * kk : 64 * h + 4 * kk]
    sum_narrow(2)
    for h in range(2):
        piece = first[:, 64 * h + 3 * kk : 64 * h + 4 * kk]
        matrix[8 * h : 8 * h + 8, 2 * kk : 3 * kk] = piece * BASIS_SCALE
    second = sum_done(1)
    for g in range(4):
        piece = second[:, 2 * kk * g : 2 * kk * (g + 1)]
        matrix[2 * kk + 4 * g : 2 * kk + 4 * g + 4, kk : 3 * kk] = piece
        matrix[kk + 4 * g : kk + 4 * g + 4, 2 * kk : 3 * kk] = piece[:, :kk]
    pick_rows = lax.broadcasted_iota(jnp.int32, (2 * kk, 128), 0)
    pick_lanes = lax.broadcasted_iota(jnp.int32, (2 * kk, 128), 1)
    pick = jnp.where(pick_lanes == pick_rows + kk, 1.0, 0.0)
    matrix[2 * kk :, 0 : 2 * kk] = dot_nt(pick, matrix[kk : 3 * kk])

    lane = lax.broadcasted_iota(jnp.int32, (1, 128), 1)

    def eliminate(system, row, k):
        shape = system.shape
        c0 = jnp.broadcast_to(system[:, k : k + 1], shape)
        c1 = jnp.broadcast_to(system[:, k + 1 : k + 2], shape)
        p0, p1 = system[row : row + 1], system[row + 1 : row + 2]
        a, b = c0[row : row + 1], c1[row : row + 1]
        c, d = c0[row + 1 : row + 2], c1[row + 1 : row + 2]
        inverse = 1.0 / (a * d - b * c)
        at0, at1 = lane == k, lane == k + 1
        g0 = jnp.where(at0, -d, jnp.where(at1, b, d * p0 - b * p1)) * inverse
        g1 = jnp.where(at0, c, jnp.where(at1, -a, a * p1 - c * p0)) * inverse
        kept = jnp.where(at0 | at1, 0.0, system)
        return kept - c0 * g0 - c1 * g1

    system = matrix[...]
    for k in range(0, 2 * kk, 2):
        system = eliminate(system, kk + k, k)

    third = sum_done(2)
    third = jnp.concatenate(
        [
            pltpu.roll(jnp.broadcast_to(third[h : h + 1], (8, 128)), 0, 1, stride=kk, stride_axis=0)
            for h in range(2)
        ],
        axis=0,
    )
    third = jnp.where((lanes >= 2 * kk) & (lanes < 3 * kk), third, 0.0)
    system = jnp.concatenate([system[:kk], system[3 * kk :] + third], axis=0)
    for k in range(0, kk, 2):
        system = eliminate(system, kk + k, 2 * kk + k)
    weights[...] = system[:kk]


def combine(weights, rhs, split, sol_hbm, res_hbm, sol, res, sol_turned, res_turned, out_sem):
    cx, cy, kk, nz = rhs.shape
    y = weights[:, : BASIS * kk]
    high = y.astype(jnp.bfloat16)
    low = (y - high.astype(F32)).astype(jnp.bfloat16)
    factors = jnp.concatenate(
        [jnp.concatenate([high, high], axis=1), jnp.concatenate([low, jnp.zeros_like(low)], axis=1)], axis=0
    )

    def weighted(at, x, yy):
        out = lax.dot_general(
            factors, split[at, x, yy], (((1,), (0,)), ((), ())), preferred_element_type=F32
        )
        return out[:kk] + out[kk:]

    copies = []
    for x in range(cx):
        for yy in range(cy):
            sol[x, yy] = weighted(0, x, yy)
            res[x, yy] = rhs[x, yy] - weighted(1, x, yy)
        for buffer, turned, target in ((sol, sol_turned, sol_hbm), (res, res_turned, res_hbm)):
            turned[x] = jnp.swapaxes(buffer[x], 0, 1)
            copy = pltpu.make_async_copy(turned.at[x], target.at[:, x], out_sem.at[len(copies)])
            copy.start()
            copies.append(copy)
    for copy in copies:
        copy.wait()


def solution(mesh):
    n_wide, n_narrow = mesh.shape["wide"], mesh.shape["narrow"]

    def on_device(sources, well_columns, column_active, perm_root, storage_term, inverse_blocks):
        kk, cx, cy, nz = sources.shape
        nb, blk = inverse_blocks.shape[2], inverse_blocks.shape[3]
        dma = pltpu.SemaphoreType.DMA
        vmem = pltpu.VMEM
        held = pl.pallas_call(
            functools.partial(kernel, n_wide, n_narrow),
            out_shape=(
                vmem((kk, 128), F32),
                vmem((cx, cy, kk, nz), F32),
                vmem((2, cx, cy, 2 * BASIS * kk, nz), jnp.bfloat16),
            ),
            in_specs=[pl.BlockSpec(memory_space=pl.ANY)] * 6,
            out_specs=(pl.BlockSpec(memory_space=vmem),) * 3,
            scratch_shapes=[
                pltpu.SMEM(well_columns.shape, jnp.int32),
                pltpu.SMEM(column_active.shape, jnp.int32),
                vmem((cx, cy, nz), F32),
                vmem((cx, cy, nz), F32),
                vmem(inverse_blocks.shape, inverse_blocks.dtype),
                vmem((cx, cy, nz), F32),
                vmem((2, cx, cy, nz), F32),
                vmem((2, cy, nz), F32),
                vmem((cx + 2, cy + 2, 8, nz), F32),
                vmem((cx, cy, nz), F32),
                vmem((BASIS, cx, cy, kk, nz), F32),
                vmem((BASIS, cx, cy, kk, nz), F32),
                vmem((BASIS, 2, cy, kk, nz), F32),
                vmem((BASIS, 2, cx, kk, nz), F32),
                *(
                    vmem(shape, F32)
                    for height in (8, 4, 2)
                    for shape in (
                        (height, 128),
                        (n_wide - 1, height, 128),
                        (height, 128),
                        (n_narrow - 1, height, 128),
                    )
                ),
                vmem(((BASIS + 1) * kk, 128), F32),
                vmem((cx, cy, 8, nz), F32),
                dma((4 + CHUNKS * cx + cx * cy,)),
                dma((4,)),
                dma((4,)),
                dma((BASIS, 2 + 2 * CHUNKS)),
                dma((BASIS, 2 + 2 * CHUNKS)),
                dma((3, 2)),
                dma((3, 2)),
                pltpu.SemaphoreType.REGULAR((2, 4)),
            ],
            compiler_params=pltpu.CompilerParams(collective_id=0, has_side_effects=True),
        )(sources, well_columns, column_active, perm_root, storage_term, inverse_blocks)
        field = jax.ShapeDtypeStruct(sources.shape, F32)
        return pl.pallas_call(
            combine,
            out_shape=(field, field),
            in_specs=[pl.BlockSpec(memory_space=vmem)] * 3,
            out_specs=(pl.BlockSpec(memory_space=pl.ANY),) * 2,
            scratch_shapes=[
                vmem((cx, cy, kk, nz), F32),
                vmem((cx, cy, kk, nz), F32),
                vmem((cx, kk, cy, nz), F32),
                vmem((cx, kk, cy, nz), F32),
                dma((2 * cx,)),
            ],
        )(*(pltpu.with_memory_space_constraint(value, vmem) for value in held))

    in_specs = (
        P(None, "wide", "narrow", None),
        P(),
        P("wide", "narrow"),
        P("wide", "narrow", None),
        P("wide", "narrow", None),
        P("wide", "narrow", None, None, None),
    )
    out_specs = (P(None, "wide", "narrow", None), P(None, "wide", "narrow", None))
    return jax.shard_map(
        on_device, mesh=mesh, in_specs=in_specs, out_specs=out_specs, check_vma=False
    )
```
